768 devices in a mesh: lat: 128 (over x, y, z_lo), grow: 6 (over z_hi, core).
Axes of the slice: x: 4, y: 8, z: 12 (z_hi: 3, z_lo: 4; z = z_hi * 4 + z_lo), core: 2. Of those that a mesh axis runs over, the one named last changes fastest.
Arguments:
- phase: float32 [96, 512, 1536], P('grow', 'lat'), may hold values from -1 to 1
- solute: float32 [96, 512, 1536], P('grow', 'lat'), may hold values from -3 to 3
- seed_grain: int32 [1536], replicated, may hold values 0 or 1
- writer: int32 [6, 128], replicated, may hold values from 0 to 127, each once within a row
Outputs:
- phase_out: float32 [96, 512, 1536], P('grow', 'lat')
- solute_out: float32 [96, 512, 1536], P('grow', 'lat')
- checkpoint: float32 [6, 128, 2, 4, 1, 64], P('grow', 'lat')
The draws below stay inside these ranges and needn't reach their ends.
Inputs may be any that keep to these rules, and one draw needn't show every extreme that they name: Each row of writer is a permutation of 0 to 127.
All inputs are finite; a program needn't handle non-finite values.
Results may differ from the reference program's by a relative error of at most 0.0003.
Values sent between devices are 32-bit elements; how exact they have to be, the bound alone decides.
No kernel may reach another device: no remote copies, remote signals or barrier semaphores. Data moves between devices by JAX's collectives and lax.ppermute only.
A program may use at most 32 MiB of HBM per device.

```python
import jax
import jax.numpy as jnp
from jax import lax

CX = 4
NY = 1536
SHIFT = 16
NX = 512
NZ = 96
WRITERS = 128
GROUPS = 6


def place_ends(values, rng, least, largest):
    longest = values.shape.index(max(values.shape))
    spots = []
    for shift in (0, 1):
        where = [jax.random.randint(jax.random.fold_in(rng, axis), (), 0, length) for axis, length in enumerate(values.shape)]
        where[longest] = (where[longest] + shift) % values.shape[longest]
        spots.append(tuple(where))
    return values.at[spots[0]].set(least).at[spots[1]].set(largest)


def shard_levels(stream_key, extent, shards, smallest, top_value):
    level = 1.0
    for axis_at, shards_of in shards:
        draws = jax.random.uniform(jax.random.fold_in(jax.random.fold_in(stream_key, 6), axis_at), (shards_of,), jnp.float32, smallest / len(shards), top_value / len(shards))
        level = level * jnp.repeat(jnp.exp(draws), extent[axis_at] // shards_of).reshape((-1,) + (1,) * (len(extent) - 1 - axis_at))
    return level


def bell_draw(stream_key, dims, spread, bound, cuts=(), held_as=jnp.bfloat16):
    gain = shard_levels(stream_key, dims, cuts, -0.22, 0.18) if cuts else 1.0
    entries = jax.random.normal(stream_key, dims, jnp.float32) * spread * gain
    return jnp.minimum(jnp.maximum(entries, -bound), bound).astype(held_as)


def setup_inputs(seed: int = 0) -> dict:
    splits = jax.random.split(jax.random.key(seed), 5)
    phase = jnp.clip(jax.random.uniform(splits[0], (NZ, NX, NY), jnp.float32, -1.0, 1.0) * shard_levels(splits[0], (NZ, NX, NY), ((0, 6), (1, 128)), -0.4, 0.0), -1.0, 1.0)
    solute = bell_draw(splits[1], (NZ, NX, NY), 0.5, 3.0, ((0, 6), (1, 128)), jnp.float32)
    seed_grain = place_ends((jax.random.randint(splits[2], (NY,), 0, 2) < 1).astype(jnp.int32), jax.random.fold_in(splits[2], 1), 0, 1)
    writer = jax.vmap(lambda own: jax.random.permutation(own, WRITERS))(jax.random.split(splits[3], GROUPS)).reshape((GROUPS, WRITERS)).astype(jnp.int32)
    return dict(phase=phase, solute=solute, seed_grain=seed_grain, writer=writer)


time_step = 0.15
aniso_strength = 0.15
coupling = 3.0
partition = 0.15
grad_floor = 0.25
solid_u = -0.5
liquid_u = 0.0
half_root = 0.7071067811865476


def advance(ext, grain, theta):
    phi_e = ext[0]
    sol_e = ext[1]
    p = phi_e[1:-1, 1:-1]
    pzp = phi_e[2:, 1:-1]
    pzm = phi_e[:-2, 1:-1]
    pxp = phi_e[1:-1, 2:]
    pxm = phi_e[1:-1, :-2]
    pyp = jnp.roll(p, -1, 2)
    pym = jnp.roll(p, 1, 2)
    grad_z = 0.5 * (pzp - pzm)
    grad_x = 0.5 * (pxp - pxm)
    grad_y = 0.5 * (pyp - pym)
    turned_x = (grad_x + grad_y) * half_root
    turned_y = (grad_x - grad_y) * half_root
    comp_x = jnp.where(grain, turned_x, grad_x)
    comp_y = jnp.where(grain, turned_y, grad_y)
    sq_x = comp_x * comp_x
    sq_y = comp_y * comp_y
    sq_z = grad_z * grad_z
    total_sq = sq_x + sq_y + sq_z
    quartic = sq_x * sq_x + sq_y * sq_y + sq_z * sq_z
    floored = jnp.maximum(total_sq, grad_floor)
    aniso = 1.0 + aniso_strength * (4.0 * quartic / (floored * floored) - 3.0)
    aniso_sq = aniso * aniso
    laplace = pzp + pzm + pxp + pxm + pyp + pym - 6.0 * p
    u = sol_e[1:-1, 1:-1]
    drive = p - p * p * p - coupling * (1.0 - p * p) ** 2 * (u + theta[:, None, None])
    rate = (aniso_sq * laplace + drive) / aniso_sq
    q_e = 0.5 * (1.0 - jnp.clip(phi_e, -1.0, 1.0))
    q = q_e[1:-1, 1:-1]
    uzp = sol_e[2:, 1:-1]
    uzm = sol_e[:-2, 1:-1]
    uxp = sol_e[1:-1, 2:]
    uxm = sol_e[1:-1, :-2]
    uyp = jnp.roll(u, -1, 2)
    uym = jnp.roll(u, 1, 2)
    flux = 0.5 * (q + q_e[2:, 1:-1]) * (uzp - u)
    flux = flux + 0.5 * (q + q_e[:-2, 1:-1]) * (uzm - u)
    flux = flux + 0.5 * (q + q_e[1:-1, 2:]) * (uxp - u)
    flux = flux + 0.5 * (q + q_e[1:-1, :-2]) * (uxm - u)
    flux = flux + 0.5 * (q + jnp.roll(q, -1, 2)) * (uyp - u)
    flux = flux + 0.5 * (q + jnp.roll(q, 1, 2)) * (uym - u)
    weight = 0.5 * (1.0 + partition - (1.0 - partition) * jnp.clip(p, -1.0, 1.0))
    urate = (flux + 0.5 * (1.0 + (1.0 - partition) * u) * rate) / weight
    return jnp.stack([p + time_step * rate, u + time_step * urate])


def full_step(state, grain, theta):
    wide = jnp.concatenate([state[:, :, -1:], state, state[:, :, :1]], axis=2)
    shape_plane = (1, 1, wide.shape[2], wide.shape[3])
    bottom = jnp.concatenate([jnp.full(shape_plane, 1.0, jnp.float32), jnp.full(shape_plane, solid_u, jnp.float32)], axis=0)
    top = jnp.concatenate([jnp.full(shape_plane, -1.0, jnp.float32), jnp.full(shape_plane, liquid_u, jnp.float32)], axis=0)
    padded = jnp.concatenate([bottom, wide, top], axis=1)
    block = 8
    count = state.shape[1] // block

    def one_block(index):
        start = (index * block).astype(jnp.int32)
        ext = lax.dynamic_slice_in_dim(padded, start, block + 2, axis=1)
        local_theta = lax.dynamic_slice_in_dim(theta, start, block, axis=0)
        return advance(ext, grain, local_theta)

    pieces = lax.map(one_block, jnp.arange(count, dtype=jnp.int32))
    pieces = jnp.moveaxis(pieces, 0, 1)
    return pieces.reshape(state.shape)


def reference(phase, solute, seed_grain, writer):
    grain = seed_grain > 0
    state = jnp.stack([phase, solute])
    theta = (jnp.arange(NZ).astype(jnp.float32) + 0.5) / NZ - 0.5
    for turn in range(2):
        state = full_step(state, grain, theta)
    lower = state[:, :SHIFT]
    coarse = lower.reshape(2, SHIFT // 4, 4, NX // 4, 4, NY // 4, 4).mean(axis=(2, 4, 6))
    fill = jnp.concatenate([jnp.full((1, SHIFT, NX, NY), -1.0, jnp.float32), jnp.full((1, SHIFT, NX, NY), liquid_u, jnp.float32)], axis=0)
    moved = jnp.concatenate([state[:, SHIFT:], fill], axis=1)
    piece = NY // (4 * GROUPS)
    blocks = coarse.reshape(2, SHIFT // 4, WRITERS, CX // 4, GROUPS, piece)
    blocks = jnp.transpose(blocks, (4, 2, 0, 1, 3, 5))
    rows = jnp.arange(GROUPS).astype(jnp.int32)[:, None] + jnp.zeros((GROUPS, WRITERS), jnp.int32)
    checkpoint = jnp.zeros(blocks.shape, jnp.float32).at[rows, writer].set(blocks)
    return moved[0], moved[1], checkpoint
```

```python
import jax
import jax.numpy as jnp
from jax import lax
from jax.sharding import PartitionSpec as P

SHIFT = 16


time_step = 0.15
aniso_strength = 0.15
coupling = 3.0
partition = 0.15
grad_floor = 0.25
solid_u = -0.5
liquid_u = 0.0
half_root = 0.7071067811865476


def advance(ext, grain, theta):
    phi_e = ext[0]
    sol_e = ext[1]
    p = phi_e[1:-1, 1:-1]
    pzp = phi_e[2:, 1:-1]
    pzm = phi_e[:-2, 1:-1]
    pxp = phi_e[1:-1, 2:]
    pxm = phi_e[1:-1, :-2]
    pyp = jnp.roll(p, -1, 2)
    pym = jnp.roll(p, 1, 2)
    grad_z = 0.5 * (pzp - pzm)
    grad_x = 0.5 * (pxp - pxm)
    grad_y = 0.5 * (pyp - pym)
    turned_x = (grad_x + grad_y) * half_root
    turned_y = (grad_x - grad_y) * half_root
    comp_x = jnp.where(grain, turned_x, grad_x)
    comp_y = jnp.where(grain, turned_y, grad_y)
    sq_x = comp_x * comp_x
    sq_y = comp_y * comp_y
    sq_z = grad_z * grad_z
    total_sq = sq_x + sq_y + sq_z
    quartic = sq_x * sq_x + sq_y * sq_y + sq_z * sq_z
    floored = jnp.maximum(total_sq, grad_floor)
    aniso = 1.0 + aniso_strength * (4.0 * quartic / (floored * floored) - 3.0)
    aniso_sq = aniso * aniso
    laplace = pzp + pzm + pxp + pxm + pyp + pym - 6.0 * p
    u = sol_e[1:-1, 1:-1]
    drive = p - p * p * p - coupling * (1.0 - p * p) ** 2 * (u + theta[:, None, None])
    rate = (aniso_sq * laplace + drive) / aniso_sq
    q_e = 0.5 * (1.0 - jnp.clip(phi_e, -1.0, 1.0))
    q = q_e[1:-1, 1:-1]
    uzp = sol_e[2:, 1:-1]
    uzm = sol_e[:-2, 1:-1]
    uxp = sol_e[1:-1, 2:]
    uxm = sol_e[1:-1, :-2]
    uyp = jnp.roll(u, -1, 2)
    uym = jnp.roll(u, 1, 2)
    flux = 0.5 * (q + q_e[2:, 1:-1]) * (uzp - u)
    flux = flux + 0.5 * (q + q_e[:-2, 1:-1]) * (uzm - u)
    flux = flux + 0.5 * (q + q_e[1:-1, 2:]) * (uxp - u)
    flux = flux + 0.5 * (q + q_e[1:-1, :-2]) * (uxm - u)
    flux = flux + 0.5 * (q + jnp.roll(q, -1, 2)) * (uyp - u)
    flux = flux + 0.5 * (q + jnp.roll(q, 1, 2)) * (uym - u)
    weight = 0.5 * (1.0 + partition - (1.0 - partition) * jnp.clip(p, -1.0, 1.0))
    urate = (flux + 0.5 * (1.0 + (1.0 - partition) * u) * rate) / weight
    return jnp.stack([p + time_step * rate, u + time_step * urate])


def shift(block, axis, step):
    count = lax.axis_size(axis)
    return lax.ppermute(block, axis, [(i, (i + step) % count) for i in range(count)])


def fields(phase, solute, like):
    return jnp.stack(
        [jnp.full(like.shape[1:], phase, jnp.float32), jnp.full(like.shape[1:], solute, jnp.float32)]
    )


def pooled(state):
    planes, rows, width = state.shape[1:]
    columns = state.reshape(2, planes // 4, 4, rows, width).sum(axis=(2, 3))
    pick = jnp.arange(128)[:, None] // 4 == jnp.arange(32)[None]
    cells = jnp.einsum(
        "fzkl,lm->fzkm",
        columns.reshape(2, planes // 4, width // 128, 128),
        jnp.where(pick, 1.0 / 64.0, 0.0).astype(jnp.float32),
        precision=lax.Precision.HIGHEST,
    )
    return cells.reshape(2, planes // 4, width // 4)


def shards(phase, solute, seed_grain, writer):
    planes, rows, width = phase.shape
    grow_count = lax.axis_size("grow")
    grow_at = lax.axis_index("grow")
    lat_count = lax.axis_size("lat")
    lat_at = lax.axis_index("lat")
    total = planes * grow_count
    grain = seed_grain > 0
    state = jnp.stack([phase, solute])
    lowest = grow_at == 0
    highest = grow_at == grow_count - 1

    below = shift(state[:, -2:], "grow", 1)
    above = shift(state[:, :2], "grow", -1)
    left = shift(state[:, :, -2:], "lat", 1)
    right = shift(state[:, :, :2], "lat", -1)
    below = jnp.where(lowest, fields(1.0, solid_u, below), below)
    above = jnp.where(highest, fields(-1.0, liquid_u, above), above)
    edges = jnp.concatenate([below[:, 1:], above[:, :1]], axis=1)
    edges_left = shift(edges[:, :, -1:], "lat", 1)
    edges_right = shift(edges[:, :, :1], "lat", -1)
    pad = ((0, 0), (0, 0), (1, 0), (0, 0))
    dap = ((0, 0), (0, 0), (0, 1), (0, 0))
    low = ((0, 0), (1, 0), (0, 0), (0, 0))
    top = ((0, 0), (0, 1), (0, 0), (0, 0))
    ext = jnp.concatenate(
        [
            jnp.concatenate(
                [
                    jnp.pad(jnp.pad(edges_left[:, :1], pad), low),
                    below,
                    jnp.pad(jnp.pad(edges_right[:, :1], dap), low),
                ],
                axis=2,
            ),
            jnp.concatenate([left, state, right], axis=2),
            jnp.concatenate(
                [
                    jnp.pad(jnp.pad(edges_left[:, 1:], pad), top),
                    above,
                    jnp.pad(jnp.pad(edges_right[:, 1:], dap), top),
                ],
                axis=2,
            ),
        ],
        axis=1,
    )
    level = (grow_at * planes - 1 + jnp.arange(planes + 2, dtype=jnp.int32)).astype(jnp.float32)
    theta = (level + 0.5) / total - 0.5
    once = advance(ext, grain, theta)
    first = jnp.where(lowest, fields(1.0, solid_u, once[:, :1]), once[:, :1])
    last = jnp.where(highest, fields(-1.0, liquid_u, once[:, -1:]), once[:, -1:])
    state = advance(jnp.concatenate([first, once[:, 1:-1], last], axis=1), grain, theta[1:-1])

    arrived = lax.ppermute(state, "grow", [(i, i - 1) for i in range(1, grow_count)])
    moved = jnp.where(highest, fields(-1.0, liquid_u, arrived), arrived)

    coarse = pooled(state)
    piece = width // 4 // grow_count
    blocks = [
        jnp.concatenate(
            [coarse[0, :, r * piece : (r + 1) * piece], coarse[1, :, r * piece : (r + 1) * piece]], axis=1
        )
        for r in range(grow_count)
    ]
    mine = jnp.where(lowest, blocks[0], 0.0)
    for r in range(1, grow_count):
        mine = mine + lax.ppermute(blocks[r], "grow", [(0, r)])
    row_ids = lax.dynamic_index_in_dim(writer, grow_at, 0, keepdims=False)
    target = lax.dynamic_index_in_dim(row_ids, lat_at, 0, keepdims=False)
    slots = jnp.where((jnp.arange(lat_count) == target)[:, None, None], mine[None], 0.0)
    landed = lax.all_to_all(slots, "lat", 0, 0, tiled=True).sum(axis=0)
    landed = jnp.stack([landed[:, :piece], landed[:, piece:]])
    return (moved[0], moved[1], landed[None, None, :, :, None])


def solution(mesh):
    placed = (P("grow", "lat", None), P("grow", "lat", None), P(), P())
    return jax.shard_map(
        shards,
        mesh=mesh,
        in_specs=placed,
        out_specs=(
            P("grow", "lat", None),
            P("grow", "lat", None),
            P("grow", "lat", None, None, None, None),
        ),
        check_vma=False,
    )
```

```python
import jax
import jax.numpy as jnp
from jax import lax
from jax.sharding import PartitionSpec as P


time_step = 0.15
aniso_strength = 0.15
coupling = 3.0
partition = 0.15
grad_floor = 0.25
solid_u = -0.5
liquid_u = 0.0
half_root = 0.7071067811865476


def advance(ext, grain, theta):
    phi_e = ext[0]
    sol_e = ext[1]
    p = phi_e[1:-1, 1:-1]
    pzp = phi_e[2:, 1:-1]
    pzm = phi_e[:-2, 1:-1]
    pxp = phi_e[1:-1, 2:]
    pxm = phi_e[1:-1, :-2]
    pyp = jnp.roll(p, -1, 2)
    pym = jnp.roll(p, 1, 2)
    grad_z = 0.5 * (pzp - pzm)
    grad_x = 0.5 * (pxp - pxm)
    grad_y = 0.5 * (pyp - pym)
    turned_x = (grad_x + grad_y) * half_root
    turned_y = (grad_x - grad_y) * half_root
    comp_x = jnp.where(grain, turned_x, grad_x)
    comp_y = jnp.where(grain, turned_y, grad_y)
    sq_x = comp_x * comp_x
    sq_y = comp_y * comp_y
    sq_z = grad_z * grad_z
    total_sq = sq_x + sq_y + sq_z
    quartic = sq_x * sq_x + sq_y * sq_y + sq_z * sq_z
    floored = jnp.maximum(total_sq, grad_floor)
    aniso = 1.0 + aniso_strength * (4.0 * quartic / (floored * floored) - 3.0)
    aniso_sq = aniso * aniso
    laplace = pzp + pzm + pxp + pxm + pyp + pym - 6.0 * p
    u = sol_e[1:-1, 1:-1]
    drive = p - p * p * p - coupling * (1.0 - p * p) ** 2 * (u + theta[:, None, None])
    rate = (aniso_sq * laplace + drive) / aniso_sq
    q_e = 0.5 * (1.0 - jnp.clip(phi_e, -1.0, 1.0))
    q = q_e[1:-1, 1:-1]
    uzp = sol_e[2:, 1:-1]
    uzm = sol_e[:-2, 1:-1]
    uxp = sol_e[1:-1, 2:]
    uxm = sol_e[1:-1, :-2]
    uyp = jnp.roll(u, -1, 2)
    uym = jnp.roll(u, 1, 2)
    flux = 0.5 * (q + q_e[2:, 1:-1]) * (uzp - u)
    flux = flux + 0.5 * (q + q_e[:-2, 1:-1]) * (uzm - u)
    flux = flux + 0.5 * (q + q_e[1:-1, 2:]) * (uxp - u)
    flux = flux + 0.5 * (q + q_e[1:-1, :-2]) * (uxm - u)
    flux = flux + 0.5 * (q + jnp.roll(q, -1, 2)) * (uyp - u)
    flux = flux + 0.5 * (q + jnp.roll(q, 1, 2)) * (uym - u)
    weight = 0.5 * (1.0 + partition - (1.0 - partition) * jnp.clip(p, -1.0, 1.0))
    urate = (flux + 0.5 * (1.0 + (1.0 - partition) * u) * rate) / weight
    return jnp.stack([p + time_step * rate, u + time_step * urate])


def exchange(low, high, axis):
    count = lax.axis_size(axis)
    even = lax.axis_index(axis) % 2 == 0
    inner = lax.ppermute(jnp.where(even, high, low), axis, [(i, i ^ 1) for i in range(count)])
    others = [(i, (i - 1 if i % 2 == 0 else i + 1) % count) for i in range(count)]
    outer = lax.ppermute(jnp.where(even, low, high), axis, others)
    return jnp.where(even, outer, inner), jnp.where(even, inner, outer)


def fields(phase, solute, like):
    return jnp.stack(
        [jnp.full(like.shape[1:], phase, jnp.float32), jnp.full(like.shape[1:], solute, jnp.float32)]
    )


def pooled(state):
    planes, rows, width = state.shape[1:]
    columns = state.reshape(2, planes // 4, 4, rows, width).sum(axis=(2, 3))
    pick = jnp.arange(128)[:, None] // 4 == jnp.arange(32)[None]
    cells = jnp.einsum(
        "fzkl,lm->fzkm",
        columns.reshape(2, planes // 4, width // 128, 128),
        jnp.where(pick, 1.0 / 64.0, 0.0).astype(jnp.float32),
        precision=lax.Precision.HIGHEST,
    )
    return cells.reshape(2, planes // 4, width // 4)


def work(phase, solute, seed_grain, writer):
    planes, _, width = phase.shape
    grow_count = lax.axis_size("grow")
    grow_at = lax.axis_index("grow")
    lat_count = lax.axis_size("lat")
    lat_at = lax.axis_index("lat")
    total = planes * grow_count
    grain = seed_grain > 0
    state = jnp.stack([phase, solute])
    lowest = grow_at == 0
    highest = grow_at == grow_count - 1

    below, above = exchange(state[:, :2], state[:, -2:], "grow")
    below = jnp.where(lowest, fields(1.0, solid_u, below), below)
    above = jnp.where(highest, fields(-1.0, liquid_u, above), above)
    tall = jnp.concatenate([below[:, 1:], state, above[:, :1]], axis=1)
    left, right = exchange(tall[:, :, :2], tall[:, :, -2:], "lat")
    pad = ((0, 0), (0, 0), (2, 2), (0, 0))
    ext = jnp.concatenate(
        [jnp.pad(below[:, :1], pad), jnp.concatenate([left, tall, right], axis=2), jnp.pad(above[:, 1:], pad)],
        axis=1,
    )
    level = (grow_at * planes - 1 + jnp.arange(planes + 2, dtype=jnp.int32)).astype(jnp.float32)
    theta = (level + 0.5) / total - 0.5
    once = advance(ext, grain, theta)
    first = jnp.where(lowest, fields(1.0, solid_u, once[:, :1]), once[:, :1])
    last = jnp.where(highest, fields(-1.0, liquid_u, once[:, -1:]), once[:, -1:])
    state = advance(jnp.concatenate([first, once[:, 1:-1], last], axis=1), grain, theta[1:-1])

    arrived = lax.ppermute(state, "grow", [(i, i - 1) for i in range(1, grow_count)])
    moved = jnp.where(highest, fields(-1.0, liquid_u, arrived), arrived)

    coarse = pooled(state)
    piece = width // 4 // grow_count
    blocks = [
        jnp.concatenate(
            [coarse[0, :, r * piece : (r + 1) * piece], coarse[1, :, r * piece : (r + 1) * piece]], axis=1
        )
        for r in range(grow_count)
    ]
    mine = jnp.where(lowest, blocks[0], 0.0)
    for r in range(1, grow_count):
        mine = mine + lax.ppermute(blocks[r], "grow", [(0, r)])
    row_ids = lax.dynamic_index_in_dim(writer, grow_at, 0, keepdims=False)
    target = lax.dynamic_index_in_dim(row_ids, lat_at, 0, keepdims=False)
    slots = jnp.where((jnp.arange(lat_count) == target)[:, None, None], mine[None], 0.0)
    landed = lax.all_to_all(slots, "lat", 0, 0, tiled=True).sum(axis=0)
    landed = jnp.stack([landed[:, :piece], landed[:, piece:]])
    return (moved[0], moved[1], landed[None, None, :, :, None])


def solution(mesh):
    placed = (P("grow", "lat", None), P("grow", "lat", None), P(), P())
    return jax.shard_map(
        work,
        mesh=mesh,
        in_specs=placed,
        out_specs=(
            P("grow", "lat", None),
            P("grow", "lat", None),
            P("grow", "lat", None, None, None, None),
        ),
        check_vma=False,
    )
```

```python
import jax
import jax.numpy as jnp
from jax import lax
from jax.sharding import Mesh
from jax.sharding import PartitionSpec as P


LAT = ("x", "y", "z")


time_step = 0.15
aniso_strength = 0.15
coupling = 3.0
partition = 0.15
grad_floor = 0.25
solid_u = -0.5
liquid_u = 0.0
half_root = 0.7071067811865476


def advance(ext, grain, theta):
    phi_e = ext[0]
    sol_e = ext[1]
    p = phi_e[1:-1, 1:-1]
    pzp = phi_e[2:, 1:-1]
    pzm = phi_e[:-2, 1:-1]
    pxp = phi_e[1:-1, 2:]
    pxm = phi_e[1:-1, :-2]
    pyp = jnp.roll(p, -1, 2)
    pym = jnp.roll(p, 1, 2)
    grad_z = 0.5 * (pzp - pzm)
    grad_x = 0.5 * (pxp - pxm)
    grad_y = 0.5 * (pyp - pym)
    turned_x = (grad_x + grad_y) * half_root
    turned_y = (grad_x - grad_y) * half_root
    comp_x = jnp.where(grain, turned_x, grad_x)
    comp_y = jnp.where(grain, turned_y, grad_y)
    sq_x = comp_x * comp_x
    sq_y = comp_y * comp_y
    sq_z = grad_z * grad_z
    total_sq = sq_x + sq_y + sq_z
    quartic = sq_x * sq_x + sq_y * sq_y + sq_z * sq_z
    floored = jnp.maximum(total_sq, grad_floor)
    aniso = 1.0 + aniso_strength * (4.0 * quartic / (floored * floored) - 3.0)
    aniso_sq = aniso * aniso
    laplace = pzp + pzm + pxp + pxm + pyp + pym - 6.0 * p
    u = sol_e[1:-1, 1:-1]
    drive = p - p * p * p - coupling * (1.0 - p * p) ** 2 * (u + theta[:, None, None])
    rate = (aniso_sq * laplace + drive) / aniso_sq
    q_e = 0.5 * (1.0 - jnp.clip(phi_e, -1.0, 1.0))
    q = q_e[1:-1, 1:-1]
    uzp = sol_e[2:, 1:-1]
    uzm = sol_e[:-2, 1:-1]
    uxp = sol_e[1:-1, 2:]
    uxm = sol_e[1:-1, :-2]
    uyp = jnp.roll(u, -1, 2)
    uym = jnp.roll(u, 1, 2)
    flux = 0.5 * (q + q_e[2:, 1:-1]) * (uzp - u)
    flux = flux + 0.5 * (q + q_e[:-2, 1:-1]) * (uzm - u)
    flux = flux + 0.5 * (q + q_e[1:-1, 2:]) * (uxp - u)
    flux = flux + 0.5 * (q + q_e[1:-1, :-2]) * (uxm - u)
    flux = flux + 0.5 * (q + jnp.roll(q, -1, 2)) * (uyp - u)
    flux = flux + 0.5 * (q + jnp.roll(q, 1, 2)) * (uym - u)
    weight = 0.5 * (1.0 + partition - (1.0 - partition) * jnp.clip(p, -1.0, 1.0))
    urate = (flux + 0.5 * (1.0 + (1.0 - partition) * u) * rate) / weight
    return jnp.stack([p + time_step * rate, u + time_step * urate])


def shift(block, axis, step):
    count = lax.axis_size(axis)
    return lax.ppermute(block, axis, [(i, (i + step) % count) for i in range(count)])


def fields(phase, solute, like):
    return jnp.stack(
        [jnp.full(like.shape[1:], phase, jnp.float32), jnp.full(like.shape[1:], solute, jnp.float32)]
    )


def pooled(state):
    planes, rows, width = state.shape[1:]
    columns = state.reshape(2, planes // 4, 4, rows, width).sum(axis=(2, 3))
    pick = jnp.arange(128)[:, None] // 4 == jnp.arange(32)[None]
    cells = jnp.einsum(
        "fzkl,lm->fzkm",
        columns.reshape(2, planes // 4, width // 128, 128),
        jnp.where(pick, 1.0 / 64.0, 0.0).astype(jnp.float32),
        precision=lax.Precision.HIGHEST,
    )
    return cells.reshape(2, planes // 4, width // 4)


def work(phase, solute, seed_grain, writer):
    planes, _, width = phase.shape
    grow_count = lax.axis_size("grow")
    grow_at = lax.axis_index("grow")
    lat_at = lax.axis_index(LAT)
    total = planes * grow_count
    grain = seed_grain > 0
    state = jnp.stack([phase, solute])
    lowest = grow_at == 0
    highest = grow_at == grow_count - 1

    left = shift(state[:, :, -2:], LAT, 1)
    right = shift(state[:, :, :2], LAT, -1)
    below = shift(state[:, -2:], "grow", 1)
    above = shift(state[:, :2], "grow", -1)
    below = jnp.where(lowest, fields(1.0, solid_u, below), below)
    above = jnp.where(highest, fields(-1.0, liquid_u, above), above)
    edges = jnp.concatenate([below[:, 1:], above[:, :1]], axis=1)
    edges_left = shift(edges[:, :, -1:], LAT, 1)
    edges_right = shift(edges[:, :, :1], LAT, -1)
    pad = ((0, 0), (0, 0), (1, 0), (0, 0))
    dap = ((0, 0), (0, 0), (0, 1), (0, 0))
    low = ((0, 0), (1, 0), (0, 0), (0, 0))
    top = ((0, 0), (0, 1), (0, 0), (0, 0))
    ext = jnp.concatenate(
        [
            jnp.concatenate(
                [
                    jnp.pad(jnp.pad(edges_left[:, :1], pad), low),
                    below,
                    jnp.pad(jnp.pad(edges_right[:, :1], dap), low),
                ],
                axis=2,
            ),
            jnp.concatenate([left, state, right], axis=2),
            jnp.concatenate(
                [
                    jnp.pad(jnp.pad(edges_left[:, 1:], pad), top),
                    above,
                    jnp.pad(jnp.pad(edges_right[:, 1:], dap), top),
                ],
                axis=2,
            ),
        ],
        axis=1,
    )
    level = (grow_at * planes - 1 + jnp.arange(planes + 2, dtype=jnp.int32)).astype(jnp.float32)
    theta = (level + 0.5) / total - 0.5
    once = advance(ext, grain, theta)
    first = jnp.where(lowest, fields(1.0, solid_u, once[:, :1]), once[:, :1])
    last = jnp.where(highest, fields(-1.0, liquid_u, once[:, -1:]), once[:, -1:])
    state = advance(jnp.concatenate([first, once[:, 1:-1], last], axis=1), grain, theta[1:-1])

    arrived = lax.ppermute(state, "grow", [(i, i - 1) for i in range(1, grow_count)])
    moved = jnp.where(highest, fields(-1.0, liquid_u, arrived), arrived)

    coarse = pooled(state)
    piece = width // 4 // grow_count
    blocks = [
        jnp.concatenate(
            [coarse[0, :, r * piece : (r + 1) * piece], coarse[1, :, r * piece : (r + 1) * piece]], axis=1
        )
        for r in range(grow_count)
    ]
    x_count, y_count, z_count = (lax.axis_size(axis) for axis in LAT)
    x_at, y_at, z_at = (lax.axis_index(axis) for axis in LAT)
    mine = jnp.stack(blocks)
    targets = lax.dynamic_index_in_dim(writer, lat_at, 1, keepdims=False)
    to_y = jnp.arange(y_count)[:, None] == (targets // z_count % y_count)[None]
    slots = jnp.where(to_y[:, :, None, None], mine[None], 0.0)
    slots = slots.reshape((y_count * grow_count,) + mine.shape[1:])
    held = lax.all_to_all(slots, ("y", "grow"), 0, 0, tiled=True)
    held = held.reshape((y_count, grow_count) + mine.shape[1:])[:, 0]
    row_ids = lax.dynamic_index_in_dim(writer, grow_at, 0, keepdims=False)
    row_ids = row_ids.reshape(x_count, y_count, z_count)
    onward = lax.dynamic_index_in_dim(row_ids, x_at, 0, keepdims=False)
    onward = lax.dynamic_index_in_dim(onward, z_at, 1, keepdims=False)
    place = onward // (y_count * z_count) * z_count + onward % z_count
    place = jnp.where(onward // z_count % y_count == y_at, place, -1)
    chosen = jnp.arange(x_count * z_count)[:, None] == place[None]
    slots = jnp.where(chosen[:, :, None, None], held[None], 0.0).sum(axis=1)
    landed = lax.all_to_all(slots, ("x", "z"), 0, 0, tiled=True).sum(axis=0)
    landed = jnp.stack([landed[:, :piece], landed[:, piece:]])
    return (moved[0], moved[1], landed[None, None, :, :, None])


def solution(mesh):
    fine = Mesh(mesh.devices.reshape(4, 8, 4, 6), LAT + ("grow",))
    placed = (P("grow", LAT, None), P("grow", LAT, None), P(), P())
    return jax.shard_map(
        work,
        mesh=fine,
        in_specs=placed,
        out_specs=(
            P("grow", LAT, None),
            P("grow", LAT, None),
            P("grow", LAT, None, None, None, None),
        ),
        check_vma=False,
    )
```

```python
import jax
import jax.numpy as jnp
from jax import lax
from jax.experimental import pallas as pl
from jax.experimental.pallas import tpu as pltpu
from jax.sharding import Mesh
from jax.sharding import PartitionSpec as P


LAT = ("x", "y", "z")
GRID = (4, 8, 4, 6)
LANES = 128

time_step = 0.15
aniso_strength = 0.15
coupling = 3.0
partition = 0.15
solid_u = -0.5
liquid_u = 0.0


def shift(block, axis, step):
    count = lax.axis_size(axis)
    return lax.ppermute(block, axis, [(i, (i + step) % count) for i in range(count)])


def clipped(p):
    return jnp.minimum(jnp.maximum(p, -1.0), 1.0)


def cell_step(p, u, near_p, near_u, theta, even_w, cross_w):
    pzp, pzm, pxp, pxm, pyp, pym = near_p
    gz = pzp - pzm
    gx = pxp - pxm
    gy = pyp - pym
    sz = gz * gz
    sx = gx * gx
    sy = gy * gy
    flat = sx + sy
    quartic = even_w * (flat * flat) + cross_w * (sx * sy) + sz * sz
    floored = jnp.maximum(flat + sz, 1.0)
    square = floored * floored
    base = 1.0 - 3.0 * aniso_strength
    ratio = square * pl.reciprocal(base * square + (4.0 * aniso_strength) * quartic, approx=False)
    laplace = ((pzp + pzm) + (pxp + pxm)) + ((pyp + pym) - 6.0 * p)
    hump = 1.0 - p * p
    drive = p * hump - (coupling * (u + theta)) * (hump * hump)
    rate = laplace + drive * (ratio * ratio)
    c = clipped(p)
    two = 2.0 - c
    flux = None
    for pn, un in zip(near_p, near_u, strict=True):
        face = (two - clipped(pn)) * (un - u)
        flux = face if flux is None else flux + face
    weight = (1.0 + partition) - (1.0 - partition) * c
    urate = (0.5 * flux + (1.0 + (1.0 - partition) * u) * rate) * pl.reciprocal(weight, approx=False)
    return p + time_step * rate, u + time_step * urate


def steps_kernel(
    at, phase, solute, left, right, below, above, edge_l, edge_r, weights, phase_to, solute_to, coarse_to,
    op, ou, dp, du, opr, our, dpr, dur, sp, su, spr, sur, tpr, tur, sums,
):
    planes, rows, width = phase.shape
    pairs = planes // 2
    last = pairs + 1
    chunks = width // LANES
    grow_at = at[0]
    lowest = grow_at == 0
    highest = grow_at == at[1] - 1
    tile = (2 * rows, LANES)
    sub = lax.broadcasted_iota(jnp.int32, tile, 0)
    lane = lax.broadcasted_iota(jnp.int32, tile, 1)
    early = sub < rows
    first_x = (sub & (rows - 1)) == 0
    last_x = (sub & (rows - 1)) == rows - 1
    first_y = lane == 0
    last_y = lane == LANES - 1
    total = (at[1] * planes).astype(jnp.float32)

    for field, (o, d, solid, liquid) in enumerate(((op, dp, 1.0, -1.0), (ou, du, solid_u, liquid_u))):
        o[0, 0:rows] = jnp.where(lowest, solid, below[field, 0])
        o[0, rows:] = jnp.where(lowest, solid, below[field, 1])
        o[last, 0:rows] = jnp.where(highest, liquid, above[field, 0])
        o[last, rows:] = jnp.where(highest, liquid, above[field, 1])
        d[0] = jnp.zeros((2 * rows, width), jnp.float32)
        d[last] = jnp.zeros((2 * rows, width), jnp.float32)
        d[0, rows : rows + 1] = jnp.where(lowest, solid, edge_r[field, 0])
        d[0, 2 * rows - 1 :] = jnp.where(lowest, solid, edge_l[field, 0])
        d[last, 0:1] = jnp.where(highest, liquid, edge_r[field, 1])
        d[last, rows - 1 : rows] = jnp.where(highest, liquid, edge_l[field, 1])

    def gather(k, carry):
        for field, (own, o, d) in enumerate(((phase, op, dp), (solute, ou, du))):
            o[k + 1, 0:rows] = own[2 * k]
            o[k + 1, rows:] = own[2 * k + 1]
            d[k + 1, 0:2] = right[field, 2 * k]
            d[k + 1, 2:4] = left[field, 2 * k]
            d[k + 1, 4:6] = right[field, 2 * k + 1]
            d[k + 1, 6:8] = left[field, 2 * k + 1]
        return carry

    lax.fori_loop(0, pairs, gather, 0)

    def turn(t, carry):
        for one, turned in ((op, opr), (ou, our), (dp, dpr), (du, dur)):
            for c in range(chunks):
                at_c = pl.ds(c * LANES, LANES)
                turned[t, :, at_c] = pltpu.roll(one[t, :, at_c], rows, 0)
        return carry

    lax.fori_loop(0, last + 1, turn, 0)

    def neighbours(one, turned, other, t, t_low, t_high, c):
        here = pl.ds(c * LANES, LANES)
        mid = one[t, :, here]
        ahead = one[t, :, pl.ds((c + 1) % chunks * LANES, LANES)]
        behind = one[t, :, pl.ds((c - 1) % chunks * LANES, LANES)]
        swapped = turned[t, :, here]
        beside = other[t, :, here]
        return mid, (
            jnp.where(early, swapped, turned[t_high, :, here]),
            jnp.where(early, turned[t_low, :, here], swapped),
            pltpu.roll(jnp.where(first_x, beside, mid), 2 * rows - 1, 0),
            pltpu.roll(jnp.where(last_x, beside, mid), 1, 0),
            pltpu.roll(jnp.where(first_y, ahead, mid), LANES - 1, 1),
            pltpu.roll(jnp.where(last_y, behind, mid), 1, 1),
        )

    def theta_of(t):
        level = (grow_at * planes + 2 * (t - 1) + jnp.where(early, 0, 1)).astype(jnp.float32)
        return (level + 0.5) / total - 0.5

    def tile_step(fields_p, fields_u, t, t_low, t_high, theta, c):
        p, near_p = neighbours(*fields_p, t, t_low, t_high, c)
        u, near_u = neighbours(*fields_u, t, t_low, t_high, c)
        here = pl.ds(c * LANES, LANES)
        return cell_step(p, u, near_p, near_u, theta, weights[0, :, here], weights[1, :, here])

    def own_once(t, carry):
        theta = theta_of(t)
        t_low = jnp.maximum(t - 1, 0)
        t_high = jnp.minimum(t + 1, last)
        solid = jnp.logical_and(lowest, t == 0)
        liquid = jnp.logical_and(highest, t == last)
        for c in range(chunks):
            here = pl.ds(c * LANES, LANES)
            p, u = tile_step((op, opr, dpr), (ou, our, dur), t, t_low, t_high, theta, c)
            p = jnp.where(solid, 1.0, jnp.where(liquid, -1.0, p))
            u = jnp.where(solid, solid_u, jnp.where(liquid, liquid_u, u))
            sp[t, :, here] = p
            su[t, :, here] = u
            spr[t, :, here] = pltpu.roll(p, rows, 0)
            sur[t, :, here] = pltpu.roll(u, rows, 0)
        return carry

    lax.fori_loop(0, last + 1, own_once, 0)

    def side_once(t, carry):
        theta = theta_of(t)
        for c in range(chunks):
            here = pl.ds(c * LANES, LANES)
            p, u = tile_step((dp, dpr, opr), (du, dur, our), t, t - 1, t + 1, theta, c)
            tpr[t, :, here] = pltpu.roll(p, rows, 0)
            tur[t, :, here] = pltpu.roll(u, rows, 0)
        return carry

    lax.fori_loop(1, last, side_once, 0)

    def own_twice(k, carry):
        t = k + 1
        theta = theta_of(t)
        for c in range(chunks):
            here = pl.ds(c * LANES, LANES)
            p, u = tile_step((sp, spr, tpr), (su, sur, tur), t, t - 1, t + 1, theta, c)
            sums[0, k, c : c + 1] = jnp.sum(p, axis=0, keepdims=True)
            sums[1, k, c : c + 1] = jnp.sum(u, axis=0, keepdims=True)
            p = jnp.where(lowest, -1.0, p)
            u = jnp.where(lowest, liquid_u, u)
            phase_to[2 * k, :, here] = p[:rows]
            phase_to[2 * k + 1, :, here] = p[rows:]
            solute_to[2 * k, :, here] = u[:rows]
            solute_to[2 * k + 1, :, here] = u[rows:]
        return carry

    lax.fori_loop(0, pairs, own_twice, 0)

    pieces = coarse_to.shape[0]
    per = chunks // pieces
    span = per * LANES
    pick = (
        lax.broadcasted_iota(jnp.int32, (LANES, LANES), 0) // 4
        - lax.broadcasted_iota(jnp.int32, (LANES, LANES), 1)
    )
    wide = LANES // 4
    total_cells = None
    for field in range(2):
        for h in range(per):
            start = field * (span // 4) + h * wide
            take = jnp.where(pick == -start, 1.0 / 64.0, 0.0).astype(jnp.float32)
            lines = []
            for r in range(pieces):
                for q in range(pairs // 2):
                    c = r * per + h
                    lines.append(sums[field, 2 * q, c : c + 1] + sums[field, 2 * q + 1, c : c + 1])
            got = jnp.dot(
                jnp.concatenate(lines, axis=0),
                take,
                precision=lax.Precision.HIGHEST,
                preferred_element_type=jnp.float32,
            )
            total_cells = got if total_cells is None else total_cells + got
    for r in range(pieces):
        coarse_to[r] = total_cells[r * (pairs // 2) : (r + 1) * (pairs // 2)]


def two_steps(at, phase, solute, left, right, below, above, edge_l, edge_r, weights, pieces, interpret=False):
    planes, rows, width = phase.shape
    pairs = planes // 2
    vmem = pl.BlockSpec(memory_space=pltpu.VMEM)
    scratch = pltpu.VMEM((pairs + 2, 2 * rows, width), jnp.float32)
    return pl.pallas_call(
        steps_kernel,
        out_shape=(
            jax.ShapeDtypeStruct(phase.shape, jnp.float32),
            jax.ShapeDtypeStruct(phase.shape, jnp.float32),
            jax.ShapeDtypeStruct((pieces, pairs // 2, LANES), jnp.float32),
        ),
        in_specs=[pl.BlockSpec(memory_space=pltpu.SMEM)] + [vmem] * 9,
        out_specs=(vmem, vmem, vmem),
        scratch_shapes=[scratch] * 14 + [pltpu.VMEM((2, pairs, width // LANES, LANES), jnp.float32)],
        interpret=interpret,
    )(at, phase, solute, left, right, below, above, edge_l, edge_r, weights)


def work(phase, solute, seed_grain, writer):
    _, rows, width = phase.shape
    grow_count = lax.axis_size("grow")
    grow_at = lax.axis_index("grow")
    lat_at = lax.axis_index(LAT)
    x_count, y_count, z_count = (lax.axis_size(axis) for axis in LAT)
    x_at, y_at, z_at = (lax.axis_index(axis) for axis in LAT)
    state = jnp.stack([phase, solute])

    below = shift(state[:, -2:], "grow", 1)
    above = shift(state[:, :2], "grow", -1)
    left = shift(state[:, :, -2:], LAT, 1)
    right = shift(state[:, :, :2], LAT, -1)
    edges = jnp.concatenate([below[:, 1:], above[:, :1]], axis=1)
    edge_l = shift(edges[:, :, -1:], LAT, 1)
    edge_r = shift(edges[:, :, :1], LAT, -1)

    turned = seed_grain > 0
    weights = jnp.stack([jnp.where(turned, 0.5, 1.0), jnp.where(turned, 2.0, -2.0)]).astype(jnp.float32)
    weights = jnp.broadcast_to(weights[:, None], (2, 2 * rows, width))
    at = jnp.stack([grow_at, jnp.int32(grow_count)]).astype(jnp.int32)
    phase_to, solute_to, blocks = two_steps(
        at, phase, solute, left, right, below, above, edge_l, edge_r, weights, grow_count
    )
    phase_out = shift(phase_to, "grow", -1)
    solute_out = shift(solute_to, "grow", -1)

    mine = jnp.where(grow_at == 0, blocks[0], 0.0)
    for r in range(1, grow_count):
        mine = mine + lax.ppermute(blocks[r], "grow", [(0, r)])
    row_ids = lax.dynamic_index_in_dim(writer, grow_at, 0, keepdims=False)
    target = lax.dynamic_index_in_dim(row_ids, lat_at, 0, keepdims=False)
    to_y = jnp.arange(y_count) == target // z_count % y_count
    slots = jnp.where(to_y[:, None, None], mine[None], 0.0)
    held = lax.all_to_all(slots, "y", 0, 0, tiled=True)
    row_ids = row_ids.reshape(x_count, y_count, z_count)
    onward = lax.dynamic_index_in_dim(row_ids, x_at, 0, keepdims=False)
    onward = lax.dynamic_index_in_dim(onward, z_at, 1, keepdims=False)
    place = onward // (y_count * z_count) * z_count + onward % z_count
    place = jnp.where(onward // z_count % y_count == y_at, place, -1)
    chosen = jnp.arange(x_count * z_count)[:, None] == place[None]
    slots = jnp.where(chosen[:, :, None, None], held[None], 0.0).sum(axis=1)
    landed = lax.all_to_all(slots, ("x", "z"), 0, 0, tiled=True).sum(axis=0)
    piece = width // 4 // grow_count
    landed = jnp.stack([landed[:, :piece], landed[:, piece:]])
    return (phase_out, solute_out, landed[None, None, :, :, None])


def solution(mesh):
    fine = Mesh(mesh.devices.reshape(GRID), LAT + ("grow",))
    placed = (P("grow", LAT, None), P("grow", LAT, None), P(), P())
    return jax.shard_map(
        work,
        mesh=fine,
        in_specs=placed,
        out_specs=(
            P("grow", LAT, None),
            P("grow", LAT, None),
            P("grow", LAT, None, None, None, None),
        ),
        check_vma=False,
    )
```

```python
import jax
import jax.numpy as jnp
from jax import lax
from jax.experimental import pallas as pl
from jax.experimental.pallas import tpu as pltpu
from jax.sharding import Mesh
from jax.sharding import PartitionSpec as P


LAT = ("x", "y", "z")
GRID = (4, 8, 4, 6)
LANES = 128

time_step = 0.15
aniso_strength = 0.15
coupling = 3.0
partition = 0.15
solid_u = -0.5
liquid_u = 0.0


def shift(block, axis, step):
    count = lax.axis_size(axis)
    return lax.ppermute(block, axis, [(i, (i + step) % count) for i in range(count)])


def near(block):
    return pltpu.with_memory_space_constraint(block, pltpu.VMEM)


def clipped(p):
    return jnp.minimum(jnp.maximum(p, -1.0), 1.0)


def cell_step(p, u, near_p, near_u, theta, even_w, cross_w):
    pzp, pzm, pxp, pxm, pyp, pym = near_p
    gz = pzp - pzm
    gx = pxp - pxm
    gy = pyp - pym
    sz = gz * gz
    sx = gx * gx
    sy = gy * gy
    flat = sx + sy
    quartic = even_w * (flat * flat) + cross_w * (sx * sy) + sz * sz
    floored = jnp.maximum(flat + sz, 1.0)
    square = floored * floored
    base = 1.0 - 3.0 * aniso_strength
    ratio = square * pl.reciprocal(base * square + (4.0 * aniso_strength) * quartic, approx=False)
    laplace = ((pzp + pzm) + (pxp + pxm)) + ((pyp + pym) - 6.0 * p)
    hump = 1.0 - p * p
    drive = p * hump - (coupling * (u + theta)) * (hump * hump)
    rate = laplace + drive * (ratio * ratio)
    c = clipped(p)
    two = 2.0 - c
    flux = None
    for pn, un in zip(near_p, near_u, strict=True):
        face = (two - clipped(pn)) * (un - u)
        flux = face if flux is None else flux + face
    weight = (1.0 + partition) - (1.0 - partition) * c
    urate = (0.5 * flux + (1.0 + (1.0 - partition) * u) * rate) * pl.reciprocal(weight, approx=False)
    return p + time_step * rate, u + time_step * urate


def steps_kernel(
    at, phase, solute, left, right, below, above, edge_l, edge_r, weights, state_to, coarse_to,
    op, ou, dp, du, opr, our, dpr, dur, sp, su, spr, sur, tpr, tur, sums,
):
    planes, rows, width = phase.shape
    pairs = planes // 2
    last = pairs + 1
    chunks = width // LANES
    grow_at = at[0]
    lowest = grow_at == 0
    highest = grow_at == at[1] - 1
    tile = (2 * rows, LANES)
    sub = lax.broadcasted_iota(jnp.int32, tile, 0)
    lane = lax.broadcasted_iota(jnp.int32, tile, 1)
    early = sub < rows
    first_x = (sub & (rows - 1)) == 0
    last_x = (sub & (rows - 1)) == rows - 1
    first_y = lane == 0
    last_y = lane == LANES - 1
    total = (at[1] * planes).astype(jnp.float32)

    for field, (o, d, solid, liquid) in enumerate(((op, dp, 1.0, -1.0), (ou, du, solid_u, liquid_u))):
        o[0, 0:rows] = jnp.where(lowest, solid, below[field, 0])
        o[0, rows:] = jnp.where(lowest, solid, below[field, 1])
        o[last, 0:rows] = jnp.where(highest, liquid, above[field, 0])
        o[last, rows:] = jnp.where(highest, liquid, above[field, 1])
        d[0] = jnp.zeros((2 * rows, width), jnp.float32)
        d[last] = jnp.zeros((2 * rows, width), jnp.float32)
        d[0, rows : rows + 1] = jnp.where(lowest, solid, edge_r[field, 0])
        d[0, 2 * rows - 1 :] = jnp.where(lowest, solid, edge_l[field, 0])
        d[last, 0:1] = jnp.where(highest, liquid, edge_r[field, 1])
        d[last, rows - 1 : rows] = jnp.where(highest, liquid, edge_l[field, 1])

    def gather(k, carry):
        for field, (own, o, d) in enumerate(((phase, op, dp), (solute, ou, du))):
            o[k + 1, 0:rows] = own[2 * k]
            o[k + 1, rows:] = own[2 * k + 1]
            d[k + 1, 0:2] = right[field, 2 * k]
            d[k + 1, 2:4] = left[field, 2 * k]
            d[k + 1, 4:6] = right[field, 2 * k + 1]
            d[k + 1, 6:8] = left[field, 2 * k + 1]
        return carry

    lax.fori_loop(0, pairs, gather, 0)

    def turn(t, carry):
        for one, turned in ((op, opr), (ou, our), (dp, dpr), (du, dur)):
            for c in range(chunks):
                at_c = pl.ds(c * LANES, LANES)
                turned[t, :, at_c] = pltpu.roll(one[t, :, at_c], rows, 0)
        return carry

    lax.fori_loop(0, last + 1, turn, 0)

    def neighbours(one, turned, other, t, t_low, t_high, c):
        here = pl.ds(c * LANES, LANES)
        mid = one[t, :, here]
        ahead = one[t, :, pl.ds((c + 1) % chunks * LANES, LANES)]
        behind = one[t, :, pl.ds((c - 1) % chunks * LANES, LANES)]
        swapped = turned[t, :, here]
        beside = other[t, :, here]
        return mid, (
            jnp.where(early, swapped, turned[t_high, :, here]),
            jnp.where(early, turned[t_low, :, here], swapped),
            pltpu.roll(jnp.where(first_x, beside, mid), 2 * rows - 1, 0),
            pltpu.roll(jnp.where(last_x, beside, mid), 1, 0),
            pltpu.roll(jnp.where(first_y, ahead, mid), LANES - 1, 1),
            pltpu.roll(jnp.where(last_y, behind, mid), 1, 1),
        )

    def theta_of(t):
        level = (grow_at * planes + 2 * (t - 1) + jnp.where(early, 0, 1)).astype(jnp.float32)
        return (level + 0.5) / total - 0.5

    def tile_step(fields_p, fields_u, t, t_low, t_high, theta, c):
        p, near_p = neighbours(*fields_p, t, t_low, t_high, c)
        u, near_u = neighbours(*fields_u, t, t_low, t_high, c)
        here = pl.ds(c * LANES, LANES)
        return cell_step(p, u, near_p, near_u, theta, weights[0:1, here], weights[1:2, here])

    def own_once(t, carry):
        theta = theta_of(t)
        t_low = jnp.maximum(t - 1, 0)
        t_high = jnp.minimum(t + 1, last)
        solid = jnp.logical_and(lowest, t == 0)
        liquid = jnp.logical_and(highest, t == last)
        for c in range(chunks):
            here = pl.ds(c * LANES, LANES)
            p, u = tile_step((op, opr, dpr), (ou, our, dur), t, t_low, t_high, theta, c)
            p = jnp.where(solid, 1.0, jnp.where(liquid, -1.0, p))
            u = jnp.where(solid, solid_u, jnp.where(liquid, liquid_u, u))
            sp[t, :, here] = p
            su[t, :, here] = u
            spr[t, :, here] = pltpu.roll(p, rows, 0)
            sur[t, :, here] = pltpu.roll(u, rows, 0)
        return carry

    lax.fori_loop(0, last + 1, own_once, 0)

    def side_once(t, carry):
        theta = theta_of(t)
        for c in range(chunks):
            here = pl.ds(c * LANES, LANES)
            p, u = tile_step((dp, dpr, opr), (du, dur, our), t, t - 1, t + 1, theta, c)
            tpr[t, :, here] = pltpu.roll(p, rows, 0)
            tur[t, :, here] = pltpu.roll(u, rows, 0)
        return carry

    lax.fori_loop(1, last, side_once, 0)

    def own_twice(k, carry):
        t = k + 1
        theta = theta_of(t)
        for c in range(chunks):
            here = pl.ds(c * LANES, LANES)
            p, u = tile_step((sp, spr, tpr), (su, sur, tur), t, t - 1, t + 1, theta, c)
            sums[0, k, c : c + 1] = jnp.sum(p, axis=0, keepdims=True)
            sums[1, k, c : c + 1] = jnp.sum(u, axis=0, keepdims=True)
            state_to[0, 2 * k, :, here] = p[:rows]
            state_to[0, 2 * k + 1, :, here] = p[rows:]
            state_to[1, 2 * k, :, here] = u[:rows]
            state_to[1, 2 * k + 1, :, here] = u[rows:]
        return carry

    lax.fori_loop(0, pairs, own_twice, 0)

    pieces = coarse_to.shape[0]
    per = chunks // pieces
    span = per * LANES
    pick = (
        lax.broadcasted_iota(jnp.int32, (LANES, LANES), 0) // 4
        - lax.broadcasted_iota(jnp.int32, (LANES, LANES), 1)
    )
    wide = LANES // 4
    total_cells = None
    for field in range(2):
        for h in range(per):
            start = field * (span // 4) + h * wide
            take = jnp.where(pick == -start, 1.0 / 64.0, 0.0).astype(jnp.float32)
            lines = []
            for r in range(pieces):
                for q in range(pairs // 2):
                    c = r * per + h
                    lines.append(sums[field, 2 * q, c : c + 1] + sums[field, 2 * q + 1, c : c + 1])
            got = jnp.dot(
                jnp.concatenate(lines, axis=0),
                take,
                precision=lax.Precision.HIGHEST,
                preferred_element_type=jnp.float32,
            )
            total_cells = got if total_cells is None else total_cells + got
    for r in range(pieces):
        coarse_to[r] = total_cells[r * (pairs // 2) : (r + 1) * (pairs // 2)]


def two_steps(at, phase, solute, left, right, below, above, edge_l, edge_r, weights, pieces, interpret=False):
    planes, rows, width = phase.shape
    pairs = planes // 2
    vmem = pl.BlockSpec(memory_space=pltpu.VMEM)
    scratch = pltpu.VMEM((pairs + 2, 2 * rows, width), jnp.float32)
    return pl.pallas_call(
        steps_kernel,
        out_shape=(
            jax.ShapeDtypeStruct((2,) + phase.shape, jnp.float32),
            jax.ShapeDtypeStruct((pieces, pairs // 2, LANES), jnp.float32),
        ),
        in_specs=[pl.BlockSpec(memory_space=pltpu.SMEM)] + [vmem] * 9,
        out_specs=(vmem, vmem),
        scratch_shapes=[scratch] * 14 + [pltpu.VMEM((2, pairs, width // LANES, LANES), jnp.float32)],
        interpret=interpret,
    )(at, phase, solute, left, right, below, above, edge_l, edge_r, weights)


def work(phase, solute, seed_grain, writer):
    _, _, width = phase.shape
    grow_count = lax.axis_size("grow")
    grow_at = lax.axis_index("grow")
    lat_at = lax.axis_index(LAT)
    lat_count = lax.axis_size(LAT)
    state = jnp.stack([phase, solute])

    below = shift(state[:, -2:], "grow", 1)
    above = shift(state[:, :2], "grow", -1)
    left = shift(state[:, :, -2:], LAT, 1)
    right = shift(state[:, :, :2], LAT, -1)
    edges = jnp.concatenate([below[:, 1:], above[:, :1]], axis=1)
    edge_l = shift(edges[:, :, -1:], LAT, 1)
    edge_r = shift(edges[:, :, :1], LAT, -1)

    turned = seed_grain > 0
    weights = jnp.stack([jnp.where(turned, 0.5, 1.0), jnp.where(turned, 2.0, -2.0)]).astype(jnp.float32)
    at = jnp.stack([grow_at, jnp.int32(grow_count)]).astype(jnp.int32)
    halos = tuple(near(halo) for halo in (left, right, below, above, edge_l, edge_r))
    state, blocks = two_steps(at, phase, solute, *halos, weights, grow_count)

    odd = lax.ppermute(blocks[1::2], "grow", [(0, 1)])
    rows_of = jnp.where(grow_at == 0, blocks[0::2], odd)
    mine = jnp.where(grow_at < 2, rows_of[0], 0.0)
    for step in range(1, grow_count // 2):
        mine = mine + lax.ppermute(rows_of[step], "grow", [(0, 2 * step), (1, 2 * step + 1)])
    arrived = lax.ppermute(state, "grow", [(i, i - 1) for i in range(1, grow_count)])
    top = grow_at == grow_count - 1
    phase_out = jnp.where(top, -1.0, arrived[0])
    solute_out = jnp.where(top, liquid_u, arrived[1])
    row_ids = lax.dynamic_index_in_dim(writer, grow_at, 0, keepdims=False)
    target = lax.dynamic_index_in_dim(row_ids, lat_at, 0, keepdims=False)
    slots = jnp.where((jnp.arange(lat_count) == target)[:, None, None], mine[None], 0.0)
    landed = lax.all_to_all(slots, LAT, 0, 0, tiled=True).sum(axis=0)
    piece = width // 4 // grow_count
    landed = jnp.stack([landed[:, :piece], landed[:, piece:]])
    return (phase_out, solute_out, landed[None, None, :, :, None])


def solution(mesh):
    fine = Mesh(mesh.devices.reshape(GRID), LAT + ("grow",))
    placed = (P("grow", LAT, None), P("grow", LAT, None), P(), P())
    return jax.shard_map(
        work,
        mesh=fine,
        in_specs=placed,
        out_specs=(
            P("grow", LAT, None),
            P("grow", LAT, None),
            P("grow", LAT, None, None, None, None),
        ),
        check_vma=False,
    )
```

```python
import jax
import jax.numpy as jnp
from jax import lax
from jax.experimental import pallas as pl
from jax.experimental.pallas import tpu as pltpu
from jax.sharding import Mesh
from jax.sharding import PartitionSpec as P


LAT = ("x", "y", "z")
GRID = (4, 8, 4, 6)
LANES = 128

time_step = 0.15
aniso_strength = 0.15
coupling = 3.0
partition = 0.15
solid_u = -0.5
liquid_u = 0.0


def shift(block, axis, step):
    count = lax.axis_size(axis)
    return lax.ppermute(block, axis, [(i, (i + step) % count) for i in range(count)])


def near(block):
    return pltpu.with_memory_space_constraint(block, pltpu.VMEM)


def clipped(p):
    return jnp.minimum(jnp.maximum(p, -1.0), 1.0)


def cell_step(p, u, near_p, near_u, theta, even_w, cross_w):
    pzp, pzm, pxp, pxm, pyp, pym = near_p
    gz = pzp - pzm
    gx = pxp - pxm
    gy = pyp - pym
    sz = gz * gz
    sx = gx * gx
    sy = gy * gy
    flat = sx + sy
    quartic = even_w * (flat * flat) + cross_w * (sx * sy) + sz * sz
    floored = jnp.maximum(flat + sz, 1.0)
    square = floored * floored
    base = 1.0 - 3.0 * aniso_strength
    ratio = square * pl.reciprocal(base * square + (4.0 * aniso_strength) * quartic, approx=False)
    laplace = ((pzp + pzm) + (pxp + pxm)) + ((pyp + pym) - 6.0 * p)
    hump = 1.0 - p * p
    drive = p * hump - (coupling * (u + theta)) * (hump * hump)
    rate = laplace + drive * (ratio * ratio)
    c = clipped(p)
    two = 2.0 - c
    flux = None
    for pn, un in zip(near_p, near_u, strict=True):
        face = (two - clipped(pn)) * (un - u)
        flux = face if flux is None else flux + face
    weight = (1.0 + partition) - (1.0 - partition) * c
    urate = (0.5 * flux + (1.0 + (1.0 - partition) * u) * rate) * pl.reciprocal(weight, approx=False)
    return p + time_step * rate, u + time_step * urate


def steps_kernel(
    at, phase, solute, left, right, below, above, edge_l, edge_r, weights, state_to, coarse_to,
    op, ou, dp, du, opr, our, dpr, dur, sp, su, spr, sur, tpr, tur, sums,
):
    planes, rows, width = phase.shape
    pairs = planes // 2
    last = pairs + 1
    chunks = width // LANES
    grow_at = at[0]
    lowest = grow_at == 0
    highest = grow_at == at[1] - 1
    tile = (2 * rows, LANES)
    sub = lax.broadcasted_iota(jnp.int32, tile, 0)
    lane = lax.broadcasted_iota(jnp.int32, tile, 1)
    early = sub < rows
    first_x = (sub & (rows - 1)) == 0
    last_x = (sub & (rows - 1)) == rows - 1
    first_y = lane == 0
    last_y = lane == LANES - 1
    total = (at[1] * planes).astype(jnp.float32)

    for field, (o, d, solid, liquid) in enumerate(((op, dp, 1.0, -1.0), (ou, du, solid_u, liquid_u))):
        o[0, 0:rows] = jnp.where(lowest, solid, below[field, 0])
        o[0, rows:] = jnp.where(lowest, solid, below[field, 1])
        o[last, 0:rows] = jnp.where(highest, liquid, above[field, 0])
        o[last, rows:] = jnp.where(highest, liquid, above[field, 1])
        d[0] = jnp.zeros((2 * rows, width), jnp.float32)
        d[last] = jnp.zeros((2 * rows, width), jnp.float32)
        d[0, rows : rows + 1] = jnp.where(lowest, solid, edge_r[field, 0])
        d[0, 2 * rows - 1 :] = jnp.where(lowest, solid, edge_l[field, 0])
        d[last, 0:1] = jnp.where(highest, liquid, edge_r[field, 1])
        d[last, rows - 1 : rows] = jnp.where(highest, liquid, edge_l[field, 1])

    def gather(k, carry):
        for field, (own, o, d) in enumerate(((phase, op, dp), (solute, ou, du))):
            o[k + 1, 0:rows] = own[2 * k]
            o[k + 1, rows:] = own[2 * k + 1]
            d[k + 1, 0:2] = right[field, 2 * k]
            d[k + 1, 2:4] = left[field, 2 * k]
            d[k + 1, 4:6] = right[field, 2 * k + 1]
            d[k + 1, 6:8] = left[field, 2 * k + 1]
        return carry

    lax.fori_loop(0, pairs, gather, 0)

    def turn(t, carry):
        for one, turned in ((op, opr), (ou, our), (dp, dpr), (du, dur)):
            for c in range(chunks):
                at_c = pl.ds(c * LANES, LANES)
                turned[t, :, at_c] = pltpu.roll(one[t, :, at_c], rows, 0)
        return carry

    lax.fori_loop(0, last + 1, turn, 0)

    def neighbours(one, turned, other, t, t_low, t_high, c):
        here = pl.ds(c * LANES, LANES)
        mid = one[t, :, here]
        ahead = one[t, :, pl.ds((c + 1) % chunks * LANES, LANES)]
        behind = one[t, :, pl.ds((c - 1) % chunks * LANES, LANES)]
        swapped = turned[t, :, here]
        beside = other[t, :, here]
        return mid, (
            jnp.where(early, swapped, turned[t_high, :, here]),
            jnp.where(early, turned[t_low, :, here], swapped),
            pltpu.roll(jnp.where(first_x, beside, mid), 2 * rows - 1, 0),
            pltpu.roll(jnp.where(last_x, beside, mid), 1, 0),
            pltpu.roll(jnp.where(first_y, ahead, mid), LANES - 1, 1),
            pltpu.roll(jnp.where(last_y, behind, mid), 1, 1),
        )

    def theta_of(t):
        level = (grow_at * planes + 2 * (t - 1) + jnp.where(early, 0, 1)).astype(jnp.float32)
        return (level + 0.5) / total - 0.5

    def tile_step(fields_p, fields_u, t, t_low, t_high, theta, c):
        p, near_p = neighbours(*fields_p, t, t_low, t_high, c)
        u, near_u = neighbours(*fields_u, t, t_low, t_high, c)
        here = pl.ds(c * LANES, LANES)
        return cell_step(p, u, near_p, near_u, theta, weights[0:1, here], weights[1:2, here])

    def own_once(t, carry):
        theta = theta_of(t)
        t_low = jnp.maximum(t - 1, 0)
        t_high = jnp.minimum(t + 1, last)
        solid = jnp.logical_and(lowest, t == 0)
        liquid = jnp.logical_and(highest, t == last)
        for c in range(chunks):
            here = pl.ds(c * LANES, LANES)
            p, u = tile_step((op, opr, dpr), (ou, our, dur), t, t_low, t_high, theta, c)
            p = jnp.where(solid, 1.0, jnp.where(liquid, -1.0, p))
            u = jnp.where(solid, solid_u, jnp.where(liquid, liquid_u, u))
            sp[t, :, here] = p
            su[t, :, here] = u
            spr[t, :, here] = pltpu.roll(p, rows, 0)
            sur[t, :, here] = pltpu.roll(u, rows, 0)
        return carry

    lax.fori_loop(0, last + 1, own_once, 0)

    def side_once(t, carry):
        theta = theta_of(t)
        for c in range(chunks):
            here = pl.ds(c * LANES, LANES)
            p, u = tile_step((dp, dpr, opr), (du, dur, our), t, t - 1, t + 1, theta, c)
            tpr[t, :, here] = pltpu.roll(p, rows, 0)
            tur[t, :, here] = pltpu.roll(u, rows, 0)
        return carry

    lax.fori_loop(1, last, side_once, 0)

    def own_twice(k, carry):
        t = k + 1
        theta = theta_of(t)
        for c in range(chunks):
            here = pl.ds(c * LANES, LANES)
            p, u = tile_step((sp, spr, tpr), (su, sur, tur), t, t - 1, t + 1, theta, c)
            sums[0, k, c : c + 1] = jnp.sum(p, axis=0, keepdims=True)
            sums[1, k, c : c + 1] = jnp.sum(u, axis=0, keepdims=True)
            state_to[0, 2 * k, :, here] = p[:rows]
            state_to[0, 2 * k + 1, :, here] = p[rows:]
            state_to[1, 2 * k, :, here] = u[:rows]
            state_to[1, 2 * k + 1, :, here] = u[rows:]
        return carry

    lax.fori_loop(0, pairs, own_twice, 0)

    pieces = coarse_to.shape[0]
    per = chunks // pieces
    span = per * LANES
    pick = (
        lax.broadcasted_iota(jnp.int32, (LANES, LANES), 0) // 4
        - lax.broadcasted_iota(jnp.int32, (LANES, LANES), 1)
    )
    wide = LANES // 4
    total_cells = None
    for field in range(2):
        for h in range(per):
            start = field * (span // 4) + h * wide
            take = jnp.where(pick == -start, 1.0 / 64.0, 0.0).astype(jnp.float32)
            lines = []
            for r in range(pieces):
                for q in range(pairs // 2):
                    c = r * per + h
                    lines.append(sums[field, 2 * q, c : c + 1] + sums[field, 2 * q + 1, c : c + 1])
            got = jnp.dot(
                jnp.concatenate(lines, axis=0),
                take,
                precision=lax.Precision.HIGHEST,
                preferred_element_type=jnp.float32,
            )
            total_cells = got if total_cells is None else total_cells + got
    for r in range(pieces):
        coarse_to[r] = total_cells[r * (pairs // 2) : (r + 1) * (pairs // 2)]


def two_steps(at, phase, solute, left, right, below, above, edge_l, edge_r, weights, pieces, interpret=False):
    planes, rows, width = phase.shape
    pairs = planes // 2
    vmem = pl.BlockSpec(memory_space=pltpu.VMEM)
    scratch = pltpu.VMEM((pairs + 2, 2 * rows, width), jnp.float32)
    return pl.pallas_call(
        steps_kernel,
        out_shape=(
            jax.ShapeDtypeStruct((2,) + phase.shape, jnp.float32),
            jax.ShapeDtypeStruct((pieces, pairs // 2, LANES), jnp.float32),
        ),
        in_specs=[pl.BlockSpec(memory_space=pltpu.SMEM)] + [vmem] * 9,
        out_specs=(vmem, vmem),
        scratch_shapes=[scratch] * 14 + [pltpu.VMEM((2, pairs, width // LANES, LANES), jnp.float32)],
        interpret=interpret,
    )(at, phase, solute, left, right, below, above, edge_l, edge_r, weights)


def work(phase, solute, seed_grain, writer):
    _, _, width = phase.shape
    grow_count = lax.axis_size("grow")
    grow_at = lax.axis_index("grow")
    lat_at = lax.axis_index(LAT)
    x_count, y_count, z_count = (lax.axis_size(axis) for axis in LAT)
    x_at, y_at, z_at = (lax.axis_index(axis) for axis in LAT)
    state = jnp.stack([phase, solute])

    below = shift(state[:, -2:], "grow", 1)
    above = shift(state[:, :2], "grow", -1)
    left = shift(state[:, :, -2:], LAT, 1)
    right = shift(state[:, :, :2], LAT, -1)
    edges = jnp.concatenate([below[:, 1:], above[:, :1]], axis=1)
    edge_l = shift(edges[:, :, -1:], LAT, 1)
    edge_r = shift(edges[:, :, :1], LAT, -1)

    turned = seed_grain > 0
    weights = jnp.stack([jnp.where(turned, 0.5, 1.0), jnp.where(turned, 2.0, -2.0)]).astype(jnp.float32)
    at = jnp.stack([grow_at, jnp.int32(grow_count)]).astype(jnp.int32)
    halos = tuple(near(halo) for halo in (left, right, below, above, edge_l, edge_r))
    state, blocks = two_steps(at, phase, solute, *halos, weights, grow_count)

    arrived = lax.ppermute(state, "grow", [(i, i - 1) for i in range(1, grow_count)])
    top = grow_at == grow_count - 1
    phase_out = jnp.where(top, -1.0, arrived[0])
    solute_out = jnp.where(top, liquid_u, arrived[1])

    targets = lax.dynamic_index_in_dim(writer, lat_at, 1, keepdims=False)
    to_y = jnp.arange(y_count)[:, None] == (targets // z_count % y_count)[None]
    slots = jnp.where(to_y[:, :, None, None], blocks[None], 0.0)
    held = lax.all_to_all(slots, "y", 0, 0, tiled=True)
    onward = writer.reshape(grow_count, x_count, y_count, z_count)
    onward = lax.dynamic_index_in_dim(onward, x_at, 1, keepdims=False)
    onward = lax.dynamic_index_in_dim(onward, z_at, 2, keepdims=False)
    place = onward // (y_count * z_count) * z_count + onward % z_count
    place = jnp.where(onward // z_count % y_count == y_at, place, -1)
    chosen = jnp.arange(x_count * z_count)[:, None, None] == place.T[None]
    slots = jnp.where(chosen[..., None, None], held[None], 0.0).sum(axis=1)
    landed = lax.all_to_all(
        slots.reshape((-1,) + slots.shape[2:]), ("x", "z", "grow"), 0, 0, tiled=True
    )
    landed = landed.reshape(slots.shape)[:, 0].sum(axis=0)
    piece = width // 4 // grow_count
    landed = jnp.stack([landed[:, :piece], landed[:, piece:]])
    return (phase_out, solute_out, landed[None, None, :, :, None])


def solution(mesh):
    fine = Mesh(mesh.devices.reshape(GRID), LAT + ("grow",))
    placed = (P("grow", LAT, None), P("grow", LAT, None), P(), P())
    return jax.shard_map(
        work,
        mesh=fine,
        in_specs=placed,
        out_specs=(
            P("grow", LAT, None),
            P("grow", LAT, None),
            P("grow", LAT, None, None, None, None),
        ),
        check_vma=False,
    )
```

```python
import jax
import jax.numpy as jnp
from jax import lax
from jax.experimental import pallas as pl
from jax.experimental.pallas import tpu as pltpu
from jax.sharding import Mesh
from jax.sharding import PartitionSpec as P


LAT = ("x", "y", "z")
GRID = (4, 8, 4, 6)
LANES = 128

time_step = 0.15
aniso_strength = 0.15
coupling = 3.0
partition = 0.15
solid_u = -0.5
liquid_u = 0.0


def shift(block, axis, step):
    count = lax.axis_size(axis)
    return lax.ppermute(block, axis, [(i, (i + step) % count) for i in range(count)])


def fields(phase, solute, like):
    return jnp.stack(
        [jnp.full(like.shape[1:], phase, jnp.float32), jnp.full(like.shape[1:], solute, jnp.float32)]
    )


def near(block):
    return pltpu.with_memory_space_constraint(block, pltpu.VMEM)


def clipped(p):
    return jnp.minimum(jnp.maximum(p, -1.0), 1.0)


def cell_step(p, u, near_p, near_u, theta, even_w, cross_w):
    pzp, pzm, pxp, pxm, pyp, pym = near_p
    gz = pzp - pzm
    gx = pxp - pxm
    gy = pyp - pym
    sz = gz * gz
    sx = gx * gx
    sy = gy * gy
    flat = sx + sy
    quartic = even_w * (flat * flat) + cross_w * (sx * sy) + sz * sz
    floored = jnp.maximum(flat + sz, 1.0)
    square = floored * floored
    base = 1.0 - 3.0 * aniso_strength
    ratio = square * pl.reciprocal(base * square + (4.0 * aniso_strength) * quartic, approx=False)
    laplace = ((pzp + pzm) + (pxp + pxm)) + ((pyp + pym) - 6.0 * p)
    hump = 1.0 - p * p
    drive = p * hump - (coupling * (u + theta)) * (hump * hump)
    rate = laplace + drive * (ratio * ratio)
    c = clipped(p)
    two = 2.0 - c
    flux = None
    for pn, un in zip(near_p, near_u, strict=True):
        face = (two - clipped(pn)) * (un - u)
        flux = face if flux is None else flux + face
    weight = (1.0 + partition) - (1.0 - partition) * c
    urate = (0.5 * flux + (1.0 + (1.0 - partition) * u) * rate) * pl.reciprocal(weight, approx=False)
    return p + time_step * rate, u + time_step * urate


def steps_kernel(
    at, phase, solute, left, right, below, above, edge_l, edge_r, weights, state_to, coarse_to,
    op, ou, dp, du, opr, our, dpr, dur, sp, su, spr, sur, tpr, tur, sums,
):
    planes, rows, width = phase.shape
    pairs = planes // 2
    last = pairs + 1
    chunks = width // LANES
    grow_at = at[0]
    lowest = grow_at == 0
    highest = grow_at == at[1] - 1
    tile = (2 * rows, LANES)
    sub = lax.broadcasted_iota(jnp.int32, tile, 0)
    lane = lax.broadcasted_iota(jnp.int32, tile, 1)
    early = sub < rows
    first_x = (sub & (rows - 1)) == 0
    last_x = (sub & (rows - 1)) == rows - 1
    first_y = lane == 0
    last_y = lane == LANES - 1
    total = (at[1] * planes).astype(jnp.float32)

    for field, (o, d, solid, liquid) in enumerate(((op, dp, 1.0, -1.0), (ou, du, solid_u, liquid_u))):
        o[0, 0:rows] = jnp.where(lowest, solid, below[field, 0])
        o[0, rows:] = jnp.where(lowest, solid, below[field, 1])
        o[last, 0:rows] = jnp.where(highest, liquid, above[field, 0])
        o[last, rows:] = jnp.where(highest, liquid, above[field, 1])
        d[0] = jnp.zeros((2 * rows, width), jnp.float32)
        d[last] = jnp.zeros((2 * rows, width), jnp.float32)
        d[0, rows : rows + 1] = edge_r[field, 0]
        d[0, 2 * rows - 1 :] = edge_l[field, 0]
        d[last, 0:1] = edge_r[field, 1]
        d[last, rows - 1 : rows] = edge_l[field, 1]

    def gather(k, carry):
        for field, (own, o, d) in enumerate(((phase, op, dp), (solute, ou, du))):
            o[k + 1, 0:rows] = own[2 * k]
            o[k + 1, rows:] = own[2 * k + 1]
            d[k + 1, 0:2] = right[field, 2 * k]
            d[k + 1, 2:4] = left[field, 2 * k]
            d[k + 1, 4:6] = right[field, 2 * k + 1]
            d[k + 1, 6:8] = left[field, 2 * k + 1]
        return carry

    lax.fori_loop(0, pairs, gather, 0)

    def turn(t, carry):
        for one, turned in ((op, opr), (ou, our), (dp, dpr), (du, dur)):
            for c in range(chunks):
                at_c = pl.ds(c * LANES, LANES)
                turned[t, :, at_c] = pltpu.roll(one[t, :, at_c], rows, 0)
        return carry

    lax.fori_loop(0, last + 1, turn, 0)

    def neighbours(one, turned, other, t, t_low, t_high, c):
        here = pl.ds(c * LANES, LANES)
        mid = one[t, :, here]
        ahead = one[t, :, pl.ds((c + 1) % chunks * LANES, LANES)]
        behind = one[t, :, pl.ds((c - 1) % chunks * LANES, LANES)]
        swapped = turned[t, :, here]
        beside = other[t, :, here]
        return mid, (
            jnp.where(early, swapped, turned[t_high, :, here]),
            jnp.where(early, turned[t_low, :, here], swapped),
            pltpu.roll(jnp.where(first_x, beside, mid), 2 * rows - 1, 0),
            pltpu.roll(jnp.where(last_x, beside, mid), 1, 0),
            pltpu.roll(jnp.where(first_y, ahead, mid), LANES - 1, 1),
            pltpu.roll(jnp.where(last_y, behind, mid), 1, 1),
        )

    def theta_of(t):
        level = (grow_at * planes + 2 * (t - 1) + jnp.where(early, 0, 1)).astype(jnp.float32)
        return (level + 0.5) / total - 0.5

    def tile_step(fields_p, fields_u, t, t_low, t_high, theta, c):
        p, near_p = neighbours(*fields_p, t, t_low, t_high, c)
        u, near_u = neighbours(*fields_u, t, t_low, t_high, c)
        here = pl.ds(c * LANES, LANES)
        return cell_step(p, u, near_p, near_u, theta, weights[0:1, here], weights[1:2, here])

    def own_once(t, carry):
        theta = theta_of(t)
        t_low = jnp.maximum(t - 1, 0)
        t_high = jnp.minimum(t + 1, last)
        solid = jnp.logical_and(lowest, t == 0)
        liquid = jnp.logical_and(highest, t == last)
        for c in range(chunks):
            here = pl.ds(c * LANES, LANES)
            p, u = tile_step((op, opr, dpr), (ou, our, dur), t, t_low, t_high, theta, c)
            p = jnp.where(solid, 1.0, jnp.where(liquid, -1.0, p))
            u = jnp.where(solid, solid_u, jnp.where(liquid, liquid_u, u))
            sp[t, :, here] = p
            su[t, :, here] = u
            spr[t, :, here] = pltpu.roll(p, rows, 0)
            sur[t, :, here] = pltpu.roll(u, rows, 0)
        return carry

    lax.fori_loop(0, last + 1, own_once, 0)

    def side_once(t, carry):
        theta = theta_of(t)
        for c in range(chunks):
            here = pl.ds(c * LANES, LANES)
            p, u = tile_step((dp, dpr, opr), (du, dur, our), t, t - 1, t + 1, theta, c)
            tpr[t, :, here] = pltpu.roll(p, rows, 0)
            tur[t, :, here] = pltpu.roll(u, rows, 0)
        return carry

    lax.fori_loop(1, last, side_once, 0)

    def own_twice(k, carry):
        t = k + 1
        theta = theta_of(t)
        for c in range(chunks):
            here = pl.ds(c * LANES, LANES)
            p, u = tile_step((sp, spr, tpr), (su, sur, tur), t, t - 1, t + 1, theta, c)
            sums[0, k, c : c + 1] = jnp.sum(p, axis=0, keepdims=True)
            sums[1, k, c : c + 1] = jnp.sum(u, axis=0, keepdims=True)
            state_to[0, 2 * k, :, here] = p[:rows]
            state_to[0, 2 * k + 1, :, here] = p[rows:]
            state_to[1, 2 * k, :, here] = u[:rows]
            state_to[1, 2 * k + 1, :, here] = u[rows:]
        return carry

    lax.fori_loop(0, pairs, own_twice, 0)

    pieces = coarse_to.shape[0]
    per = chunks // pieces
    span = per * LANES
    pick = (
        lax.broadcasted_iota(jnp.int32, (LANES, LANES), 0) // 4
        - lax.broadcasted_iota(jnp.int32, (LANES, LANES), 1)
    )
    wide = LANES // 4
    total_cells = None
    for field in range(2):
        for h in range(per):
            start = field * (span // 4) + h * wide
            take = jnp.where(pick == -start, 1.0 / 64.0, 0.0).astype(jnp.float32)
            lines = []
            for r in range(pieces):
                for q in range(pairs // 2):
                    c = r * per + h
                    lines.append(sums[field, 2 * q, c : c + 1] + sums[field, 2 * q + 1, c : c + 1])
            got = jnp.dot(
                jnp.concatenate(lines, axis=0),
                take,
                precision=lax.Precision.HIGHEST,
                preferred_element_type=jnp.float32,
            )
            total_cells = got if total_cells is None else total_cells + got
    for r in range(pieces):
        coarse_to[r] = total_cells[r * (pairs // 2) : (r + 1) * (pairs // 2)]


def two_steps(at, phase, solute, left, right, below, above, edge_l, edge_r, weights, pieces, interpret=False):
    planes, rows, width = phase.shape
    pairs = planes // 2
    vmem = pl.BlockSpec(memory_space=pltpu.VMEM)
    scratch = pltpu.VMEM((pairs + 2, 2 * rows, width), jnp.float32)
    return pl.pallas_call(
        steps_kernel,
        out_shape=(
            jax.ShapeDtypeStruct((2,) + phase.shape, jnp.float32),
            jax.ShapeDtypeStruct((pieces, pairs // 2, LANES), jnp.float32),
        ),
        in_specs=[pl.BlockSpec(memory_space=pltpu.SMEM)] + [vmem] * 9,
        out_specs=(vmem, vmem),
        scratch_shapes=[scratch] * 14 + [pltpu.VMEM((2, pairs, width // LANES, LANES), jnp.float32)],
        interpret=interpret,
    )(at, phase, solute, left, right, below, above, edge_l, edge_r, weights)


def work(phase, solute, seed_grain, writer):
    _, _, width = phase.shape
    grow_count = lax.axis_size("grow")
    grow_at = lax.axis_index("grow")
    lat_at = lax.axis_index(LAT)
    x_count, y_count, z_count = (lax.axis_size(axis) for axis in LAT)
    x_at, y_at, z_at = (lax.axis_index(axis) for axis in LAT)
    state = jnp.stack([phase, solute])

    below = shift(state[:, -2:], "grow", 1)
    above = shift(state[:, :2], "grow", -1)
    left = shift(state[:, :, -2:], LAT, 1)
    right = shift(state[:, :, :2], LAT, -1)
    lowest = grow_at == 0
    highest = grow_at == grow_count - 1
    edges = jnp.concatenate(
        [
            jnp.where(lowest, fields(1.0, solid_u, below[:, 1:]), below[:, 1:]),
            jnp.where(highest, fields(-1.0, liquid_u, above[:, :1]), above[:, :1]),
        ],
        axis=1,
    )
    edge_l = shift(edges[:, :, -1:], LAT, 1)
    edge_r = shift(edges[:, :, :1], LAT, -1)

    turned = seed_grain > 0
    weights = jnp.stack([jnp.where(turned, 0.5, 1.0), jnp.where(turned, 2.0, -2.0)]).astype(jnp.float32)
    at = jnp.stack([grow_at, jnp.int32(grow_count)]).astype(jnp.int32)
    halos = tuple(near(halo) for halo in (left, right, below, above, edge_l, edge_r))
    state, blocks = two_steps(at, phase, solute, *halos, weights, grow_count)

    odd = lax.ppermute(blocks[1::2], "grow", [(0, 1)])
    rows_of = jnp.where(grow_at == 0, blocks[0::2], odd)
    mine = jnp.where(grow_at < 2, rows_of[0], 0.0)
    for step in range(1, grow_count // 2):
        mine = mine + lax.ppermute(rows_of[step], "grow", [(0, 2 * step), (1, 2 * step + 1)])
    arrived = lax.ppermute(state, "grow", [(i, i - 1) for i in range(1, grow_count)])
    top = grow_at == grow_count - 1
    phase_out = jnp.where(top, -1.0, arrived[0])
    solute_out = jnp.where(top, liquid_u, arrived[1])
    row_ids = lax.dynamic_index_in_dim(writer, grow_at, 0, keepdims=False)
    target = lax.dynamic_index_in_dim(row_ids, lat_at, 0, keepdims=False)
    to_y = jnp.arange(y_count) == target // z_count % y_count
    slots = jnp.where(to_y[:, None, None], mine[None], 0.0)
    held = lax.all_to_all(slots, "y", 0, 0, tiled=True)
    onward = row_ids.reshape(x_count, y_count, z_count)
    onward = lax.dynamic_index_in_dim(onward, x_at, 0, keepdims=False)
    onward = lax.dynamic_index_in_dim(onward, z_at, 1, keepdims=False)
    place = onward // (y_count * z_count) * z_count + onward % z_count
    place = jnp.where(onward // z_count % y_count == y_at, place, -1)
    chosen = jnp.arange(x_count * z_count)[:, None] == place[None]
    slots = jnp.where(chosen[:, :, None, None], held[None], 0.0).sum(axis=1)
    landed = lax.all_to_all(slots, ("x", "z"), 0, 0, tiled=True).sum(axis=0)
    piece = width // 4 // grow_count
    landed = jnp.stack([landed[:, :piece], landed[:, piece:]])
    return (phase_out, solute_out, landed[None, None, :, :, None])


def solution(mesh):
    fine = Mesh(mesh.devices.reshape(GRID), LAT + ("grow",))
    placed = (P("grow", LAT, None), P("grow", LAT, None), P(), P())
    return jax.shard_map(
        work,
        mesh=fine,
        in_specs=placed,
        out_specs=(
            P("grow", LAT, None),
            P("grow", LAT, None),
            P("grow", LAT, None, None, None, None),
        ),
        check_vma=False,
    )
```

```python
import jax
import jax.numpy as jnp
from jax import lax
from jax.experimental import pallas as pl
from jax.experimental.pallas import tpu as pltpu
from jax.sharding import Mesh
from jax.sharding import PartitionSpec as P


LAT = ("x", "y", "z")
GRID = (4, 8, 4, 6)
LANES = 128

time_step = 0.15
aniso_strength = 0.15
coupling = 3.0
partition = 0.15
solid_u = -0.5
liquid_u = 0.0


def shift(block, axis, step):
    count = lax.axis_size(axis)
    return lax.ppermute(block, axis, [(i, (i + step) % count) for i in range(count)])


def fields(phase, solute, like):
    return jnp.stack(
        [jnp.full(like.shape[1:], phase, jnp.float32), jnp.full(like.shape[1:], solute, jnp.float32)]
    )


def near(block):
    return pltpu.with_memory_space_constraint(block, pltpu.VMEM)


def clipped(p):
    return jnp.minimum(jnp.maximum(p, -1.0), 1.0)


def cell_step(p, u, near_p, near_u, theta, even_w, cross_w):
    pzp, pzm, pxp, pxm, pyp, pym = near_p
    gz = pzp - pzm
    gx = pxp - pxm
    gy = pyp - pym
    sz = gz * gz
    sx = gx * gx
    sy = gy * gy
    flat = sx + sy
    quartic = even_w * (flat * flat) + cross_w * (sx * sy) + sz * sz
    floored = jnp.maximum(flat + sz, 1.0)
    square = floored * floored
    base = 1.0 - 3.0 * aniso_strength
    ratio = square * pl.reciprocal(base * square + (4.0 * aniso_strength) * quartic, approx=False)
    laplace = ((pzp + pzm) + (pxp + pxm)) + ((pyp + pym) - 6.0 * p)
    hump = 1.0 - p * p
    drive = p * hump - (coupling * (u + theta)) * (hump * hump)
    rate = laplace + drive * (ratio * ratio)
    c = clipped(p)
    two = 2.0 - c
    flux = None
    for pn, un in zip(near_p, near_u, strict=True):
        face = (two - clipped(pn)) * (un - u)
        flux = face if flux is None else flux + face
    weight = (1.0 + partition) - (1.0 - partition) * c
    urate = (0.5 * flux + (1.0 + (1.0 - partition) * u) * rate) * pl.reciprocal(weight, approx=False)
    return p + time_step * rate, u + time_step * urate


def steps_kernel(
    at, phase, solute, left, right, below, above, edge_l, edge_r, weights, state_to, slots_to,
    op, ou, dp, du, opr, our, dpr, dur, sp, su, spr, sur, tpr, tur, sums,
):
    planes, rows, width = phase.shape
    pairs = planes // 2
    last = pairs + 1
    chunks = width // LANES
    grow_at = at[0]
    lowest = grow_at == 0
    highest = grow_at == at[1] - 1
    tile = (2 * rows, LANES)
    sub = lax.broadcasted_iota(jnp.int32, tile, 0)
    lane = lax.broadcasted_iota(jnp.int32, tile, 1)
    early = sub < rows
    first_x = (sub & (rows - 1)) == 0
    last_x = (sub & (rows - 1)) == rows - 1
    first_y = lane == 0
    last_y = lane == LANES - 1
    total = (at[1] * planes).astype(jnp.float32)

    for field, (o, d, solid, liquid) in enumerate(((op, dp, 1.0, -1.0), (ou, du, solid_u, liquid_u))):
        o[0, 0:rows] = jnp.where(lowest, solid, below[field, 0])
        o[0, rows:] = jnp.where(lowest, solid, below[field, 1])
        o[last, 0:rows] = jnp.where(highest, liquid, above[field, 0])
        o[last, rows:] = jnp.where(highest, liquid, above[field, 1])
        d[0] = jnp.zeros((2 * rows, width), jnp.float32)
        d[last] = jnp.zeros((2 * rows, width), jnp.float32)
        d[0, rows : rows + 1] = edge_r[field, 0]
        d[0, 2 * rows - 1 :] = edge_l[field, 0]
        d[last, 0:1] = edge_r[field, 1]
        d[last, rows - 1 : rows] = edge_l[field, 1]

    def gather(k, carry):
        for field, (own, o, d) in enumerate(((phase, op, dp), (solute, ou, du))):
            o[k + 1, 0:rows] = own[2 * k]
            o[k + 1, rows:] = own[2 * k + 1]
            d[k + 1, 0:2] = right[field, 2 * k]
            d[k + 1, 2:4] = left[field, 2 * k]
            d[k + 1, 4:6] = right[field, 2 * k + 1]
            d[k + 1, 6:8] = left[field, 2 * k + 1]
        return carry

    lax.fori_loop(0, pairs, gather, 0)

    def turn(t, carry):
        for one, turned in ((op, opr), (ou, our), (dp, dpr), (du, dur)):
            for c in range(chunks):
                at_c = pl.ds(c * LANES, LANES)
                turned[t, :, at_c] = pltpu.roll(one[t, :, at_c], rows, 0)
        return carry

    lax.fori_loop(0, last + 1, turn, 0)

    def neighbours(one, turned, other, t, t_low, t_high, c):
        here = pl.ds(c * LANES, LANES)
        mid = one[t, :, here]
        ahead = one[t, :, pl.ds((c + 1) % chunks * LANES, LANES)]
        behind = one[t, :, pl.ds((c - 1) % chunks * LANES, LANES)]
        swapped = turned[t, :, here]
        beside = other[t, :, here]
        return mid, (
            jnp.where(early, swapped, turned[t_high, :, here]),
            jnp.where(early, turned[t_low, :, here], swapped),
            pltpu.roll(jnp.where(first_x, beside, mid), 2 * rows - 1, 0),
            pltpu.roll(jnp.where(last_x, beside, mid), 1, 0),
            pltpu.roll(jnp.where(first_y, ahead, mid), LANES - 1, 1),
            pltpu.roll(jnp.where(last_y, behind, mid), 1, 1),
        )

    def theta_of(t):
        level = (grow_at * planes + 2 * (t - 1) + jnp.where(early, 0, 1)).astype(jnp.float32)
        return (level + 0.5) / total - 0.5

    def tile_step(fields_p, fields_u, t, t_low, t_high, theta, c):
        p, near_p = neighbours(*fields_p, t, t_low, t_high, c)
        u, near_u = neighbours(*fields_u, t, t_low, t_high, c)
        here = pl.ds(c * LANES, LANES)
        return cell_step(p, u, near_p, near_u, theta, weights[0:1, here], weights[1:2, here])

    def own_once(t, carry):
        theta = theta_of(t)
        t_low = jnp.maximum(t - 1, 0)
        t_high = jnp.minimum(t + 1, last)
        solid = jnp.logical_and(lowest, t == 0)
        liquid = jnp.logical_and(highest, t == last)
        for c in range(chunks):
            here = pl.ds(c * LANES, LANES)
            p, u = tile_step((op, opr, dpr), (ou, our, dur), t, t_low, t_high, theta, c)
            p = jnp.where(solid, 1.0, jnp.where(liquid, -1.0, p))
            u = jnp.where(solid, solid_u, jnp.where(liquid, liquid_u, u))
            sp[t, :, here] = p
            su[t, :, here] = u
            spr[t, :, here] = pltpu.roll(p, rows, 0)
            sur[t, :, here] = pltpu.roll(u, rows, 0)
        return carry

    lax.fori_loop(0, last + 1, own_once, 0)

    def side_once(t, carry):
        theta = theta_of(t)
        for c in range(chunks):
            here = pl.ds(c * LANES, LANES)
            p, u = tile_step((dp, dpr, opr), (du, dur, our), t, t - 1, t + 1, theta, c)
            tpr[t, :, here] = pltpu.roll(p, rows, 0)
            tur[t, :, here] = pltpu.roll(u, rows, 0)
        return carry

    lax.fori_loop(1, last, side_once, 0)

    def own_twice(k, carry):
        t = k + 1
        theta = theta_of(t)
        for c in range(chunks):
            here = pl.ds(c * LANES, LANES)
            p, u = tile_step((sp, spr, tpr), (su, sur, tur), t, t - 1, t + 1, theta, c)
            sums[0, k, c : c + 1] = jnp.sum(p, axis=0, keepdims=True)
            sums[1, k, c : c + 1] = jnp.sum(u, axis=0, keepdims=True)
            state_to[0, 2 * k, :, here] = p[:rows]
            state_to[0, 2 * k + 1, :, here] = p[rows:]
            state_to[1, 2 * k, :, here] = u[:rows]
            state_to[1, 2 * k + 1, :, here] = u[rows:]
        return carry

    lax.fori_loop(0, pairs, own_twice, 0)

    y_count = slots_to.shape[0]
    pieces = slots_to.shape[1] * slots_to.shape[2]
    per = chunks // pieces
    span = per * LANES
    pick = (
        lax.broadcasted_iota(jnp.int32, (LANES, LANES), 0) // 4
        - lax.broadcasted_iota(jnp.int32, (LANES, LANES), 1)
    )
    wide = LANES // 4
    total_cells = None
    for field in range(2):
        for h in range(per):
            start = field * (span // 4) + h * wide
            take = jnp.where(pick == -start, 1.0 / 64.0, 0.0).astype(jnp.float32)
            lines = []
            for r in range(pieces):
                for q in range(pairs // 2):
                    c = r * per + h
                    lines.append(sums[field, 2 * q, c : c + 1] + sums[field, 2 * q + 1, c : c + 1])
            got = jnp.dot(
                jnp.concatenate(lines, axis=0),
                take,
                precision=lax.Precision.HIGHEST,
                preferred_element_type=jnp.float32,
            )
            total_cells = got if total_cells is None else total_cells + got
    for r in range(pieces):
        block = total_cells[r * (pairs // 2) : (r + 1) * (pairs // 2)]
        for y in range(y_count):
            slots_to[y, r % 2, r // 2] = jnp.where(at[2 + r] == y, block, 0.0)


def two_steps(at, phase, solute, left, right, below, above, edge_l, edge_r, weights, pieces, y_count, interpret=False):
    planes, rows, width = phase.shape
    pairs = planes // 2
    vmem = pl.BlockSpec(memory_space=pltpu.VMEM)
    scratch = pltpu.VMEM((pairs + 2, 2 * rows, width), jnp.float32)
    return pl.pallas_call(
        steps_kernel,
        out_shape=(
            jax.ShapeDtypeStruct((2,) + phase.shape, jnp.float32),
            jax.ShapeDtypeStruct((y_count, 2, pieces // 2, pairs // 2, LANES), jnp.float32),
        ),
        in_specs=[pl.BlockSpec(memory_space=pltpu.SMEM)] + [vmem] * 9,
        out_specs=(vmem, vmem),
        scratch_shapes=[scratch] * 14 + [pltpu.VMEM((2, pairs, width // LANES, LANES), jnp.float32)],
        interpret=interpret,
    )(at, phase, solute, left, right, below, above, edge_l, edge_r, weights)


def work(phase, solute, seed_grain, writer):
    _, _, width = phase.shape
    grow_count = lax.axis_size("grow")
    grow_at = lax.axis_index("grow")
    lat_at = lax.axis_index(LAT)
    x_count, y_count, z_count = (lax.axis_size(axis) for axis in LAT)
    x_at, y_at, z_at = (lax.axis_index(axis) for axis in LAT)
    state = jnp.stack([phase, solute])

    below = shift(state[:, -2:], "grow", 1)
    above = shift(state[:, :2], "grow", -1)
    left = shift(state[:, :, -2:], LAT, 1)
    right = shift(state[:, :, :2], LAT, -1)
    lowest = grow_at == 0
    highest = grow_at == grow_count - 1
    edges = jnp.concatenate(
        [
            jnp.where(lowest, fields(1.0, solid_u, below[:, 1:]), below[:, 1:]),
            jnp.where(highest, fields(-1.0, liquid_u, above[:, :1]), above[:, :1]),
        ],
        axis=1,
    )
    edge_l = shift(edges[:, :, -1:], LAT, 1)
    edge_r = shift(edges[:, :, :1], LAT, -1)

    turned = seed_grain > 0
    weights = jnp.stack([jnp.where(turned, 0.5, 1.0), jnp.where(turned, 2.0, -2.0)]).astype(jnp.float32)
    targets = lax.dynamic_index_in_dim(writer, lat_at, 1, keepdims=False)
    at = jnp.concatenate([jnp.stack([grow_at, jnp.int32(grow_count)]), targets // z_count % y_count])
    halos = tuple(near(halo) for halo in (left, right, below, above, edge_l, edge_r))
    state, slots = two_steps(at, phase, solute, *halos, weights, grow_count, y_count)

    arrived = lax.ppermute(state, "grow", [(i, i - 1) for i in range(1, grow_count)])
    top = grow_at == grow_count - 1
    phase_out = jnp.where(top, -1.0, arrived[0])
    solute_out = jnp.where(top, liquid_u, arrived[1])

    held = lax.all_to_all(slots, "y", 0, 0, tiled=True)
    odd = lax.ppermute(held[:, 1], "grow", [(0, 1)])
    rows_of = jnp.where(grow_at == 0, held[:, 0], odd)
    mine = jnp.where(grow_at < 2, rows_of[:, 0], 0.0)
    for step in range(1, grow_count // 2):
        mine = mine + lax.ppermute(rows_of[:, step], "grow", [(0, 2 * step), (1, 2 * step + 1)])
    held = mine
    row_ids = lax.dynamic_index_in_dim(writer, grow_at, 0, keepdims=False)
    onward = row_ids.reshape(x_count, y_count, z_count)
    onward = lax.dynamic_index_in_dim(onward, x_at, 0, keepdims=False)
    onward = lax.dynamic_index_in_dim(onward, z_at, 1, keepdims=False)
    place = onward // (y_count * z_count) * z_count + onward % z_count
    place = jnp.where(onward // z_count % y_count == y_at, place, -1)
    chosen = jnp.arange(x_count * z_count)[:, None] == place[None]
    slots = jnp.where(chosen[:, :, None, None], held[None], 0.0).sum(axis=1)
    landed = lax.all_to_all(slots, ("x", "z"), 0, 0, tiled=True).sum(axis=0)
    piece = width // 4 // grow_count
    landed = jnp.stack([landed[:, :piece], landed[:, piece:]])
    return (phase_out, solute_out, landed[None, None, :, :, None])


def solution(mesh):
    fine = Mesh(mesh.devices.reshape(GRID), LAT + ("grow",))
    placed = (P("grow", LAT, None), P("grow", LAT, None), P(), P())
    return jax.shard_map(
        work,
        mesh=fine,
        in_specs=placed,
        out_specs=(
            P("grow", LAT, None),
            P("grow", LAT, None),
            P("grow", LAT, None, None, None, None),
        ),
        check_vma=False,
    )
```

```python
import jax
import jax.numpy as jnp
from jax import lax
from jax.experimental import pallas as pl
from jax.experimental.pallas import tpu as pltpu
from jax.sharding import Mesh
from jax.sharding import PartitionSpec as P


LAT = ("x", "y", "z")
GRID = (4, 8, 4, 6)
LANES = 128
RELAYED = 384

time_step = 0.15
aniso_strength = 0.15
coupling = 3.0
partition = 0.15
solid_u = -0.5
liquid_u = 0.0


def shift(block, axis, step):
    count = lax.axis_size(axis)
    return lax.ppermute(block, axis, [(i, (i + step) % count) for i in range(count)])


def fields(phase, solute, like):
    return jnp.stack(
        [jnp.full(like.shape[1:], phase, jnp.float32), jnp.full(like.shape[1:], solute, jnp.float32)]
    )


def near(block):
    return pltpu.with_memory_space_constraint(block, pltpu.VMEM)


def clipped(p):
    return jnp.minimum(jnp.maximum(p, -1.0), 1.0)


def cell_step(p, u, near_p, near_u, theta, even_w, cross_w):
    pzp, pzm, pxp, pxm, pyp, pym = near_p
    gz = pzp - pzm
    gx = pxp - pxm
    gy = pyp - pym
    sz = gz * gz
    sx = gx * gx
    sy = gy * gy
    flat = sx + sy
    quartic = even_w * (flat * flat) + cross_w * (sx * sy) + sz * sz
    floored = jnp.maximum(flat + sz, 1.0)
    square = floored * floored
    base = 1.0 - 3.0 * aniso_strength
    ratio = square * pl.reciprocal(base * square + (4.0 * aniso_strength) * quartic, approx=False)
    laplace = ((pzp + pzm) + (pxp + pxm)) + ((pyp + pym) - 6.0 * p)
    hump = 1.0 - p * p
    drive = p * hump - (coupling * (u + theta)) * (hump * hump)
    rate = laplace + drive * (ratio * ratio)
    c = clipped(p)
    two = 2.0 - c
    flux = None
    for pn, un in zip(near_p, near_u, strict=True):
        face = (two - clipped(pn)) * (un - u)
        flux = face if flux is None else flux + face
    weight = (1.0 + partition) - (1.0 - partition) * c
    urate = (0.5 * flux + (1.0 + (1.0 - partition) * u) * rate) * pl.reciprocal(weight, approx=False)
    return p + time_step * rate, u + time_step * urate


def steps_kernel(
    at, phase, solute, left, right, below, above, edge_l, edge_r, weights, direct_to, relay_to, slots_to,
    op, ou, dp, du, opr, our, dpr, dur, sp, su, spr, sur, tpr, tur, sums,
):
    planes, rows, width = phase.shape
    pairs = planes // 2
    last = pairs + 1
    chunks = width // LANES
    direct_chunks = direct_to.shape[-1] // LANES
    grow_at = at[0]
    lowest = grow_at == 0
    highest = grow_at == at[1] - 1
    tile = (2 * rows, LANES)
    sub = lax.broadcasted_iota(jnp.int32, tile, 0)
    lane = lax.broadcasted_iota(jnp.int32, tile, 1)
    early = sub < rows
    first_x = (sub & (rows - 1)) == 0
    last_x = (sub & (rows - 1)) == rows - 1
    first_y = lane == 0
    last_y = lane == LANES - 1
    total = (at[1] * planes).astype(jnp.float32)

    for field, (o, d, solid, liquid) in enumerate(((op, dp, 1.0, -1.0), (ou, du, solid_u, liquid_u))):
        o[0, 0:rows] = jnp.where(lowest, solid, below[field, 0])
        o[0, rows:] = jnp.where(lowest, solid, below[field, 1])
        o[last, 0:rows] = jnp.where(highest, liquid, above[field, 0])
        o[last, rows:] = jnp.where(highest, liquid, above[field, 1])
        d[0] = jnp.zeros((2 * rows, width), jnp.float32)
        d[last] = jnp.zeros((2 * rows, width), jnp.float32)
        d[0, rows : rows + 1] = edge_r[field, 0]
        d[0, 2 * rows - 1 :] = edge_l[field, 0]
        d[last, 0:1] = edge_r[field, 1]
        d[last, rows - 1 : rows] = edge_l[field, 1]

    def gather(k, carry):
        for field, (own, o, d) in enumerate(((phase, op, dp), (solute, ou, du))):
            o[k + 1, 0:rows] = own[2 * k]
            o[k + 1, rows:] = own[2 * k + 1]
            d[k + 1, 0:2] = right[field, 2 * k]
            d[k + 1, 2:4] = left[field, 2 * k]
            d[k + 1, 4:6] = right[field, 2 * k + 1]
            d[k + 1, 6:8] = left[field, 2 * k + 1]
        return carry

    lax.fori_loop(0, pairs, gather, 0)

    def turn(t, carry):
        for one, turned in ((op, opr), (ou, our), (dp, dpr), (du, dur)):
            for c in range(chunks):
                at_c = pl.ds(c * LANES, LANES)
                turned[t, :, at_c] = pltpu.roll(one[t, :, at_c], rows, 0)
        return carry

    lax.fori_loop(0, last + 1, turn, 0)

    def neighbours(one, turned, other, t, t_low, t_high, c):
        here = pl.ds(c * LANES, LANES)
        mid = one[t, :, here]
        ahead = one[t, :, pl.ds((c + 1) % chunks * LANES, LANES)]
        behind = one[t, :, pl.ds((c - 1) % chunks * LANES, LANES)]
        swapped = turned[t, :, here]
        beside = other[t, :, here]
        return mid, (
            jnp.where(early, swapped, turned[t_high, :, here]),
            jnp.where(early, turned[t_low, :, here], swapped),
            pltpu.roll(jnp.where(first_x, beside, mid), 2 * rows - 1, 0),
            pltpu.roll(jnp.where(last_x, beside, mid), 1, 0),
            pltpu.roll(jnp.where(first_y, ahead, mid), LANES - 1, 1),
            pltpu.roll(jnp.where(last_y, behind, mid), 1, 1),
        )

    def theta_of(t):
        level = (grow_at * planes + 2 * (t - 1) + jnp.where(early, 0, 1)).astype(jnp.float32)
        return (level + 0.5) / total - 0.5

    def tile_step(fields_p, fields_u, t, t_low, t_high, theta, c):
        p, near_p = neighbours(*fields_p, t, t_low, t_high, c)
        u, near_u = neighbours(*fields_u, t, t_low, t_high, c)
        here = pl.ds(c * LANES, LANES)
        return cell_step(p, u, near_p, near_u, theta, weights[0:1, here], weights[1:2, here])

    def own_once(t, carry):
        theta = theta_of(t)
        t_low = jnp.maximum(t - 1, 0)
        t_high = jnp.minimum(t + 1, last)
        solid = jnp.logical_and(lowest, t == 0)
        liquid = jnp.logical_and(highest, t == last)
        for c in range(chunks):
            here = pl.ds(c * LANES, LANES)
            p, u = tile_step((op, opr, dpr), (ou, our, dur), t, t_low, t_high, theta, c)
            p = jnp.where(solid, 1.0, jnp.where(liquid, -1.0, p))
            u = jnp.where(solid, solid_u, jnp.where(liquid, liquid_u, u))
            sp[t, :, here] = p
            su[t, :, here] = u
            spr[t, :, here] = pltpu.roll(p, rows, 0)
            sur[t, :, here] = pltpu.roll(u, rows, 0)
        return carry

    lax.fori_loop(0, last + 1, own_once, 0)

    def side_once(t, carry):
        theta = theta_of(t)
        for c in range(chunks):
            here = pl.ds(c * LANES, LANES)
            p, u = tile_step((dp, dpr, opr), (du, dur, our), t, t - 1, t + 1, theta, c)
            tpr[t, :, here] = pltpu.roll(p, rows, 0)
            tur[t, :, here] = pltpu.roll(u, rows, 0)
        return carry

    lax.fori_loop(1, last, side_once, 0)

    def own_twice(k, carry):
        t = k + 1
        theta = theta_of(t)
        for c in range(chunks):
            here = pl.ds(c * LANES, LANES)
            p, u = tile_step((sp, spr, tpr), (su, sur, tur), t, t - 1, t + 1, theta, c)
            sums[0, k, c : c + 1] = jnp.sum(p, axis=0, keepdims=True)
            sums[1, k, c : c + 1] = jnp.sum(u, axis=0, keepdims=True)
            straight = c < direct_chunks
            state_to = direct_to if straight else relay_to
            there = pl.ds((c if straight else c - direct_chunks) * LANES, LANES)
            state_to[0, 2 * k, :, there] = p[:rows]
            state_to[0, 2 * k + 1, :, there] = p[rows:]
            state_to[1, 2 * k, :, there] = u[:rows]
            state_to[1, 2 * k + 1, :, there] = u[rows:]
        return carry

    lax.fori_loop(0, pairs, own_twice, 0)

    y_count = slots_to.shape[0]
    pieces = slots_to.shape[1] * slots_to.shape[2]
    per = chunks // pieces
    span = per * LANES
    pick = (
        lax.broadcasted_iota(jnp.int32, (LANES, LANES), 0) // 4
        - lax.broadcasted_iota(jnp.int32, (LANES, LANES), 1)
    )
    wide = LANES // 4
    total_cells = None
    for field in range(2):
        for h in range(per):
            start = field * (span // 4) + h * wide
            take = jnp.where(pick == -start, 1.0 / 64.0, 0.0).astype(jnp.float32)
            lines = []
            for r in range(pieces):
                for q in range(pairs // 2):
                    c = r * per + h
                    lines.append(sums[field, 2 * q, c : c + 1] + sums[field, 2 * q + 1, c : c + 1])
            got = jnp.dot(
                jnp.concatenate(lines, axis=0),
                take,
                precision=lax.Precision.HIGHEST,
                preferred_element_type=jnp.float32,
            )
            total_cells = got if total_cells is None else total_cells + got
    for r in range(pieces):
        block = total_cells[r * (pairs // 2) : (r + 1) * (pairs // 2)]
        for y in range(y_count):
            slots_to[y, r % 2, r // 2] = jnp.where(at[2 + r] == y, block, 0.0)


def two_steps(at, phase, solute, left, right, below, above, edge_l, edge_r, weights, pieces, y_count, interpret=False):
    planes, rows, width = phase.shape
    pairs = planes // 2
    vmem = pl.BlockSpec(memory_space=pltpu.VMEM)
    scratch = pltpu.VMEM((pairs + 2, 2 * rows, width), jnp.float32)
    return pl.pallas_call(
        steps_kernel,
        out_shape=(
            jax.ShapeDtypeStruct((2, planes, rows, width - RELAYED), jnp.float32),
            jax.ShapeDtypeStruct((2, planes, rows, RELAYED), jnp.float32),
            jax.ShapeDtypeStruct((y_count, 2, pieces // 2, pairs // 2, LANES), jnp.float32),
        ),
        in_specs=[pl.BlockSpec(memory_space=pltpu.SMEM)] + [vmem] * 9,
        out_specs=(vmem, vmem, vmem),
        scratch_shapes=[scratch] * 14 + [pltpu.VMEM((2, pairs, width // LANES, LANES), jnp.float32)],
        interpret=interpret,
    )(at, phase, solute, left, right, below, above, edge_l, edge_r, weights)


def work(phase, solute, seed_grain, writer):
    _, _, width = phase.shape
    grow_count = lax.axis_size("grow")
    grow_at = lax.axis_index("grow")
    lat_at = lax.axis_index(LAT)
    x_count, y_count, z_count = (lax.axis_size(axis) for axis in LAT)
    x_at, y_at, z_at = (lax.axis_index(axis) for axis in LAT)
    state = jnp.stack([phase, solute])

    below = shift(state[:, -2:], "grow", 1)
    above = shift(state[:, :2], "grow", -1)
    left = shift(state[:, :, -2:], LAT, 1)
    right = shift(state[:, :, :2], LAT, -1)
    lowest = grow_at == 0
    highest = grow_at == grow_count - 1
    edges = jnp.concatenate(
        [
            jnp.where(lowest, fields(1.0, solid_u, below[:, 1:]), below[:, 1:]),
            jnp.where(highest, fields(-1.0, liquid_u, above[:, :1]), above[:, :1]),
        ],
        axis=1,
    )
    edge_l = shift(edges[:, :, -1:], LAT, 1)
    edge_r = shift(edges[:, :, :1], LAT, -1)

    turned = seed_grain > 0
    weights = jnp.stack([jnp.where(turned, 0.5, 1.0), jnp.where(turned, 2.0, -2.0)]).astype(jnp.float32)
    targets = lax.dynamic_index_in_dim(writer, lat_at, 1, keepdims=False)
    at = jnp.concatenate([jnp.stack([grow_at, jnp.int32(grow_count)]), targets // z_count % y_count])
    halos = tuple(near(halo) for halo in (left, right, below, above, edge_l, edge_r))
    direct, relayed, slots = two_steps(at, phase, solute, *halos, weights, grow_count, y_count)

    inside = [(i, i - 1) for i in range(1, grow_count, 2)]
    down = range(2, grow_count, 2)
    first_hop = [(i, (i + 3) % grow_count) for i in down]
    second_hop = [((i + 3) % grow_count, i - 1) for i in down]
    direct = lax.ppermute(direct, "grow", [(i, i - 1) for i in range(1, grow_count)])
    relayed = lax.ppermute(relayed, "grow", inside + first_hop)
    onto = lax.ppermute(relayed, "grow", second_hop)
    arrived = jnp.concatenate([direct, jnp.where(grow_at % 2 == 0, relayed, onto)], axis=-1)
    top = grow_at == grow_count - 1
    phase_out = jnp.where(top, -1.0, arrived[0])
    solute_out = jnp.where(top, liquid_u, arrived[1])

    held = lax.all_to_all(slots, "y", 0, 0, tiled=True)
    odd = lax.ppermute(held[:, 1], "grow", [(0, 1)])
    rows_of = jnp.where(grow_at == 0, held[:, 0], odd)
    mine = jnp.where(grow_at < 2, rows_of[:, 0], 0.0)
    for step in range(1, grow_count // 2):
        mine = mine + lax.ppermute(rows_of[:, step], "grow", [(0, 2 * step), (1, 2 * step + 1)])
    held = mine
    row_ids = lax.dynamic_index_in_dim(writer, grow_at, 0, keepdims=False)
    onward = row_ids.reshape(x_count, y_count, z_count)
    onward = lax.dynamic_index_in_dim(onward, x_at, 0, keepdims=False)
    onward = lax.dynamic_index_in_dim(onward, z_at, 1, keepdims=False)
    place = onward // (y_count * z_count) * z_count + onward % z_count
    place = jnp.where(onward // z_count % y_count == y_at, place, -1)
    chosen = jnp.arange(x_count * z_count)[:, None] == place[None]
    slots = jnp.where(chosen[:, :, None, None], held[None], 0.0).sum(axis=1)
    landed = lax.all_to_all(slots, ("x", "z"), 0, 0, tiled=True).sum(axis=0)
    piece = width // 4 // grow_count
    landed = jnp.stack([landed[:, :piece], landed[:, piece:]])
    return (phase_out, solute_out, landed[None, None, :, :, None])


def solution(mesh):
    fine = Mesh(mesh.devices.reshape(GRID), LAT + ("grow",))
    placed = (P("grow", LAT, None), P("grow", LAT, None), P(), P())
    return jax.shard_map(
        work,
        mesh=fine,
        in_specs=placed,
        out_specs=(
            P("grow", LAT, None),
            P("grow", LAT, None),
            P("grow", LAT, None, None, None, None),
        ),
        check_vma=False,
    )
```
